32 devices in a mesh: dp: 8 (over y, x, core), tensor: 4 (over z).
Axes of the slice: x: 2, y: 2, z: 4, core: 2. Of those that a mesh axis runs over, the one named last changes fastest.
Arguments:
- queries: bfloat16 [8, 512, 4096], P('dp', 'tensor'), may hold values from -200 to 200
- dialogue_keys: bfloat16 [8, 512, 512], P('dp', 'tensor'), may hold values from -6 to 6
- dialogue_values: bfloat16 [8, 512, 512], P('dp', 'tensor'), may hold values from -6 to 6
- out_grad: bfloat16 [8, 512, 4096], P('dp', 'tensor'), may hold values from -96 to 96
- lengths: int32 [8], P('dp'), may hold values from 128 to 512, as said below
- cartridge: float32 [1024, 2, 512], P('dp', None, 'tensor'), may hold values from -6 to 6
- first_moment: float32 [1024, 2, 512], P('dp', None, 'tensor'), may hold values from -2 to 2
- second_moment: float32 [1024, 2, 512], P('dp', None, 'tensor'), may hold values from 0.01 to 4
Outputs:
- q_grad: bfloat16 [8, 512, 4096], P('dp', 'tensor')
- key_grad: bfloat16 [8, 512, 512], P('dp', 'tensor')
- value_grad: bfloat16 [8, 512, 512], P('dp', 'tensor')
- new_cartridge: float32 [1024, 2, 512], P('dp', None, 'tensor')
- new_m: float32 [1024, 2, 512], P('dp', None, 'tensor')
- new_v: float32 [1024, 2, 512], P('dp', None, 'tensor')
The draws below stay inside these ranges and needn't reach their ends.
Inputs may be any that keep to these rules, and one draw needn't show every extreme that they name: `lengths`: each conversation's real tokens stand at its start; some conversation has exactly 512.
All inputs are finite; a program needn't handle non-finite values.
Results may differ from the reference program's by a relative error of at most 0.0079.
Values may be sent and summed in bfloat16 or wider, within the bound.
A program may use at most 64 MiB of HBM per device.

```python
import math
import jax
import jax.numpy as jnp
from jax import lax

QUERY_HEADS = 32
KEY_VALUE_HEADS = 4
HEAD_WIDTH = 128
PREFIX_TOKENS = 1024
SLOT_COUNT = 512
STEP = 10
DIALOGUE_COUNT = 8


def shared_keys(key):
    drawn = jax.random.normal(jax.random.fold_in(key, 101), (DIALOGUE_COUNT, SLOT_COUNT, KEY_VALUE_HEADS, HEAD_WIDTH), jnp.float32)
    return jnp.clip(drawn, -6.0, 6.0)


def draw_dialogue_keys(key, part):
    return shared_keys(key).reshape(DIALOGUE_COUNT, SLOT_COUNT, KEY_VALUE_HEADS * HEAD_WIDTH).astype(jnp.bfloat16)


def draw_queries(key, part):
    base = jax.random.normal(jax.random.fold_in(key, 5), (DIALOGUE_COUNT, SLOT_COUNT, QUERY_HEADS * HEAD_WIDTH), jnp.float32)
    return jnp.clip(base, -200.0, 200.0).astype(jnp.bfloat16)


def draw_lengths(key, part):
    drawn = jax.random.randint(key, (DIALOGUE_COUNT,), SLOT_COUNT // 4, SLOT_COUNT + 1)
    longest = jax.random.randint(jax.random.fold_in(key, 11), (), 0, DIALOGUE_COUNT)
    return jnp.where(jnp.arange(DIALOGUE_COUNT) == longest, SLOT_COUNT, drawn).astype(jnp.int32)


def block_levels(key, shape, shards, smallest, high):
    def one(position, parts):
        heights = jax.random.uniform(jax.random.fold_in(jax.random.fold_in(key, 6), position), (parts,), jnp.float32, smallest / len(shards), high / len(shards))
        return jnp.repeat(jnp.exp(heights), shape[position] // parts).reshape((-1,) + (1,) * (len(shape) - position - 1))

    level = one(*shards[0])
    for cut in shards[1:]:
        level = level * one(*cut)
    return level


def scatter_about(rng, extent, width, bound, shards=(), held_as=jnp.bfloat16):
    array = jax.random.normal(rng, extent, jnp.float32) * width
    if len(shards) > 0:
        array = block_levels(rng, extent, shards, -0.22, 0.18) * array
    return jnp.clip(array, min=-bound, max=bound).astype(held_as)


def setup_inputs(seed: int = 0) -> dict:
    keys = jax.random.split(jax.random.key(seed), 9)
    return {
        "queries": draw_queries(jax.random.fold_in(keys[8], 71), 0),
        "dialogue_keys": draw_dialogue_keys(jax.random.fold_in(keys[8], 71), 0),
        "dialogue_values": scatter_about(keys[2], (DIALOGUE_COUNT, SLOT_COUNT, KEY_VALUE_HEADS * HEAD_WIDTH), 1.0, 6.0, ((0, 8), (1, 4))),
        "out_grad": scatter_about(keys[3], (DIALOGUE_COUNT, SLOT_COUNT, QUERY_HEADS * HEAD_WIDTH), 16.0, 96.0, ((0, 8), (1, 4))),
        "lengths": draw_lengths(jax.random.fold_in(keys[8], 71), 0),
        "cartridge": scatter_about(keys[5], (PREFIX_TOKENS, 2, KEY_VALUE_HEADS * HEAD_WIDTH), 1.0, 6.0, ((0, 8), (2, 4)), jnp.float32),
        "first_moment": scatter_about(keys[6], (PREFIX_TOKENS, 2, KEY_VALUE_HEADS * HEAD_WIDTH), 0.3, 2.0, ((0, 8), (2, 4)), jnp.float32),
        "second_moment": jnp.clip(jnp.exp(math.log(4.0) - 5.9914646 * jax.random.uniform(keys[7], (PREFIX_TOKENS, 2, KEY_VALUE_HEADS * HEAD_WIDTH), jnp.float32) ** block_levels(keys[7], (PREFIX_TOKENS, 2, KEY_VALUE_HEADS * HEAD_WIDTH), ((0, 8), (2, 4)), -0.2, 0.2)), 0.01, 4.0),
    }


BETA_ONE = 0.9
BETA_TWO = 0.999
ADAM_EPS = 1e-08
LEARN_RATE = 0.01
MASKED = -1e+30

def head_terms(head_queries, head_grads, all_keys, all_values, score_scale):
    scores = jnp.dot(head_queries, all_keys.T, preferred_element_type=jnp.float32) * score_scale
    key_pos = jnp.arange(all_keys.shape[0]) - PREFIX_TOKENS
    row_pos = jnp.arange(head_queries.shape[0])
    scores = jnp.where(key_pos[None, :] <= row_pos[:, None], scores, MASKED)
    row_max = lax.optimization_barrier(jnp.max(scores, axis=1, keepdims=True))
    exp_scores = jnp.exp(scores - row_max)
    weights = exp_scores / lax.optimization_barrier(jnp.sum(exp_scores, axis=1, keepdims=True))
    weights_half = weights.astype(jnp.bfloat16)
    attended = jnp.dot(weights_half, all_values, preferred_element_type=jnp.float32).astype(jnp.bfloat16)
    row_dot = lax.optimization_barrier(jnp.sum(head_grads.astype(jnp.float32) * attended.astype(jnp.float32), axis=1, keepdims=True))
    weight_grad = jnp.dot(head_grads, all_values.T, preferred_element_type=jnp.float32)
    score_grad = (weights * (weight_grad - row_dot)).astype(jnp.bfloat16)
    query_grad = (jnp.dot(score_grad, all_keys, preferred_element_type=jnp.float32) * score_scale).astype(jnp.bfloat16)
    key_part = jnp.dot(score_grad.T, head_queries, preferred_element_type=jnp.float32) * score_scale
    value_part = jnp.dot(weights_half.T, head_grads, preferred_element_type=jnp.float32)
    return (query_grad, key_part, value_part)

def reference(queries, dialogue_keys, dialogue_values, out_grad, lengths, cartridge, first_moment, second_moment):
    score_scale = HEAD_WIDTH ** (-0.5)
    prefix = cartridge.astype(jnp.bfloat16)
    head_group_size = QUERY_HEADS // KEY_VALUE_HEADS
    positions = jnp.arange(SLOT_COUNT)

    def one_sample(running, inputs):
        sample_queries, sample_keys, sample_values, sample_grads, sample_length = inputs
        sample_grads = jnp.where((positions < sample_length)[:, None], sample_grads, jnp.zeros((), sample_grads.dtype))
        query_parts, key_parts, value_parts, prefix_kparts, prefix_vparts = ([], [], [], [], [])
        for head_group_index in range(KEY_VALUE_HEADS):
            columns = slice(head_group_index * HEAD_WIDTH, (head_group_index + 1) * HEAD_WIDTH)
            all_keys = jnp.concatenate([prefix[:, 0, columns], sample_keys[:, columns]], 0)
            all_values = jnp.concatenate([prefix[:, 1, columns], sample_values[:, columns]], 0)
            head_columns = slice(head_group_index * head_group_size * HEAD_WIDTH, (head_group_index + 1) * head_group_size * HEAD_WIDTH)
            head_queries = sample_queries[:, head_columns].reshape(SLOT_COUNT, head_group_size, HEAD_WIDTH).transpose(1, 0, 2)
            head_grads = sample_grads[:, head_columns].reshape(SLOT_COUNT, head_group_size, HEAD_WIDTH).transpose(1, 0, 2)
            query_grad, key_part, value_part = jax.vmap(head_terms, in_axes=(0, 0, None, None, None))(head_queries, head_grads, all_keys, all_values, score_scale)
            key_part = lax.optimization_barrier(jnp.sum(key_part, 0))
            value_part = lax.optimization_barrier(jnp.sum(value_part, 0))
            query_parts.append(query_grad.transpose(1, 0, 2).reshape(SLOT_COUNT, head_group_size * HEAD_WIDTH))
            key_parts.append(key_part[PREFIX_TOKENS:].astype(jnp.bfloat16))
            value_parts.append(value_part[PREFIX_TOKENS:].astype(jnp.bfloat16))
            prefix_kparts.append(key_part[:PREFIX_TOKENS])
            prefix_vparts.append(value_part[:PREFIX_TOKENS])
        term = jnp.stack([jnp.concatenate(prefix_kparts, 1), jnp.concatenate(prefix_vparts, 1)], 1)
        return (running + term, (jnp.concatenate(query_parts, 1), jnp.concatenate(key_parts, 1), jnp.concatenate(value_parts, 1)))
    initial_sum = jnp.zeros((PREFIX_TOKENS, 2, KEY_VALUE_HEADS * HEAD_WIDTH), jnp.float32)
    prefix_grad, (q_grad, key_grad, value_grad) = lax.scan(one_sample, initial_sum, (queries, dialogue_keys, dialogue_values, out_grad, lengths))
    new_m = BETA_ONE * first_moment + (1.0 - BETA_ONE) * prefix_grad
    new_v = BETA_TWO * second_moment + (1.0 - BETA_TWO) * prefix_grad * prefix_grad
    update = new_m / (1.0 - BETA_ONE ** STEP) / (jnp.sqrt(new_v / (1.0 - BETA_TWO ** STEP)) + ADAM_EPS)
    new_cartridge = cartridge - LEARN_RATE * update
    return (q_grad, key_grad, value_grad, new_cartridge, new_m, new_v)
```

```python
import functools
import math

import jax
import jax.numpy as jnp
from jax import lax
from jax.experimental import pallas as pl
from jax.experimental.pallas import tpu as pltpu
from jax.sharding import PartitionSpec as P

STEP = 10
BETA_ONE = 0.9
BETA_TWO = 0.999
ADAM_EPS = 1e-08
LEARN_RATE = 0.01
MASKED = -1e30
WIDTH = 128
GROUP = 4
VMEM = pltpu.VMEM
MESH = pl.DeviceIdType.MESH
F32 = jnp.float32
BF16 = jnp.bfloat16


def greet(dp_n, tp_n, me, z):
    barrier = pltpu.get_barrier_semaphore()
    for other in range(1, tp_n):
        pl.semaphore_signal(
            barrier, inc=1, device_id=(me, lax.rem(z + other, tp_n)), device_id_type=MESH
        )
    half, par = me // 2, lax.rem(me, 2)
    pl.semaphore_signal(barrier, inc=1, device_id=(2 * half + 1 - par, z), device_id_type=MESH)
    for other in range(1, dp_n // 2):
        peer = 2 * lax.rem(half + other, dp_n // 2) + par
        pl.semaphore_signal(barrier, inc=1, device_id=(peer, z), device_id_type=MESH)
    pl.semaphore_wait(barrier, tp_n - 1 + dp_n // 2)


def fused_kernel(
    dp_n, tp_n, scale, len_ref, cart_hbm, k_ref, v_ref, q_hbm, g_hbm, grad_ref, kvg_ref, qg_hbm,
    cart_ref, pre_ref, q_ref, g_ref, qg_ref, gp, gkv, keys, vals, keys_t, dk, dv, sc, ec, dc,
    dpre, ddia, pair_in, pair_sum, plane_in, plane_sum, line_in, dia_in, dia_acc,
    local, kv_local, qg_sem, pre_send, pre_recv, kv_send, kv_recv, swap_send, relay,
    pair_send, pair_recv, plane_send, plane_recv, line_send, line_recv, dia_send, dia_recv,
):
    me, z = lax.axis_index("dp"), lax.axis_index("tensor")
    half, par = me // 2, lax.rem(me, 2)
    halves = dp_n // 2
    partner = 2 * half + 1 - par
    rows = k_ref.shape[0]
    total = keys.shape[0]
    dia = tp_n * rows
    pre = total - dia
    part = pre_ref.shape[1]
    heads = q_ref.shape[1] // WIDTH // tp_n
    steps = heads // GROUP
    wide = rows * GROUP
    chunk = 512
    spans = [slice(at, at + chunk) for at in range(0, total, chunk)]

    def remote(src, dst, s, r, to):
        return pltpu.make_async_remote_copy(
            src_ref=src, dst_ref=dst, send_sem=s, recv_sem=r, device_id=to, device_id_type=MESH
        )

    def lanes(k, width):
        return pl.ds(pl.multiple_of(k * width, width), width)

    keep = [
        pltpu.make_async_copy(q_hbm, q_ref, local.at[0]),
        pltpu.make_async_copy(g_hbm, g_ref, local.at[1]),
    ] + [
        pltpu.make_async_copy(
            (k_ref, v_ref)[w].at[:, k * WIDTH : (k + 1) * WIDTH], gkv.at[k, z, w], kv_local.at[2 * k + w]
        )
        for k in range(tp_n)
        for w in range(2)
    ]
    cart_copy = pltpu.make_async_copy(cart_hbm, cart_ref, local.at[2])
    cart_copy.start()
    for copy in keep:
        copy.start()
    cart_copy.wait()
    for w in range(2):
        pre_ref[w] = cart_ref[:, w, :].astype(BF16)
    own_copy = pltpu.make_async_copy(pre_ref, gp.at[z, me], local.at[3])
    own_copy.start()
    for copy in keep[2:]:
        copy.wait()
    keep = keep[:2] + [own_copy]
    greet(dp_n, tp_n, me, z)

    bits = tp_n.bit_length() - 1

    def flip(a, b):
        out = 0
        for bit in range(bits):
            u, v = lax.rem(a // 2**bit, 2), lax.rem(b // 2**bit, 2)
            out = out + 2**bit * (u + v - 2 * u * v)
        return out

    def head_at(j):
        j = jnp.int32(j)
        return flip(z, flip(j, j // 2))

    mate = z + 1 - 2 * lax.rem(z, 2)

    def pre_across(j):
        return remote(
            pre_ref, gp.at[z, me], pre_send.at[j], pre_recv.at[z * dp_n + me], (me, head_at(j))
        )

    def pre_spread(t, j, other):
        src = pre_ref if t is z else gp.at[t, me]
        to = 2 * lax.rem(half + other, halves) + par if other else partner
        return remote(
            src, gp.at[t, me], pre_send.at[tp_n + j * halves + other], pre_recv.at[t * dp_n + me], (to, z)
        )

    def pre_relay(t, j, other):
        d = 2 * lax.rem(half + halves - other, halves) + par
        return remote(
            gp.at[t, d], gp.at[t, d], relay.at[j * halves + other], pre_recv.at[t * dp_n + d], (partner, z)
        )

    def pre_await(t, d):
        remote(gp.at[t, d], gp.at[t, d], pre_send.at[0], pre_recv.at[t * dp_n + d], (partner, z)).wait_recv()

    def kv_copy(j, other):
        j = jnp.int32(j)
        k = flip(z + other, flip(j, j // 2))
        return remote(
            gkv.at[k, z], gkv.at[k, z], kv_send.at[other * tp_n + j], kv_recv.at[k * tp_n + z], (me, z + other)
        )

    def kv_swap(k, j, b):
        return remote(gkv.at[k, b], gkv.at[k, b], swap_send.at[j * tp_n + b], kv_recv.at[k * tp_n + b], (me, mate))

    def kv_send_all(j):
        for other in range(tp_n - 1, 0, -1):

            @pl.when(z + other < tp_n)
            def _():
                kv_copy(j, other).start()

    def swap_all(k, j):
        for b in range(tp_n - 1):

            @pl.when(b < mate)
            def _():
                kv_swap(k, j, b).start()

    for other in list(range(1, halves)) + [0]:
        pre_spread(z, 0, other).start()
    if tp_n > 1:
        pre_across(1).start()
    kv_send_all(0)
    for j in range(2, tp_n):
        pre_across(j).start()

    for b in range(1, tp_n):

        @pl.when(z < b)
        def _():
            gkv[:, b] = jnp.zeros((tp_n, 2, rows, WIDTH), BF16)

    for copy in keep:
        copy.wait()

    def relay_all(t, j):
        for other in range(1, halves):
            copy = pre_relay(t, j, other)
            copy.wait_recv()
            copy.start()

    def spread_all(j):
        t = head_at(j)
        pre_await(t, me)
        for other in list(range(1, halves)) + [0]:
            pre_spread(t, j, other).start()

    if tp_n > 1:
        spread_all(1)
    relay_all(z, 0)

    real = z * rows + lax.broadcasted_iota(jnp.int32, (rows, WIDTH), 0) < len_ref[0]
    nt = (((1,), (1,)), ((), ()))
    fold = scale * math.log2(math.e)

    def attend(k, p, between):
        def cut(ref, i):
            return ref[:, lanes(k * heads + p * GROUP + i, WIDTH)]

        q = jnp.concatenate([cut(q_ref, i) for i in range(GROUP)], 0)
        g = jnp.concatenate(
            [jnp.where(real, cut(g_ref, i).astype(F32), 0.0).astype(BF16) for i in range(GROUP)], 0
        )
        top = jnp.full((1, wide), MASKED, F32)
        row_pos = z * rows + lax.rem(lax.broadcasted_iota(jnp.int32, (chunk, wide), 1), rows)
        lead = lax.broadcasted_iota(jnp.int32, (chunk, wide), 0) - row_pos
        for span in spans:
            s = lax.dot_general(keys[span], q, nt, preferred_element_type=F32)
            if span.start >= pre:
                s = jnp.where(lead <= pre - span.start, s, MASKED)
            sc[span] = s
            top = jnp.maximum(top, jnp.max(s, axis=0, keepdims=True))
        norm = jnp.zeros((1, wide), F32)
        mix = jnp.zeros((1, wide), F32)
        for span in spans:
            e = jnp.exp2((sc[span] - top) * fold)
            d = lax.dot_general(vals[span], g, nt, preferred_element_type=F32)
            norm += jnp.sum(e, axis=0, keepdims=True)
            mix += jnp.sum(e * d, axis=0, keepdims=True)
            ec[span] = e
            dc[span] = d
        inv = 1.0 / norm
        row_dot = mix * inv
        between()
        qt = jnp.zeros((WIDTH, wide), F32)
        for span in spans:
            w = ec[span] * inv
            ds = (w * (dc[span] - row_dot)).astype(BF16)
            more_v = jnp.dot(w.astype(BF16), g, preferred_element_type=F32)
            more_k = jnp.dot(ds, q, preferred_element_type=F32)
            if p == 0:
                dv[span] = more_v
                dk[span] = more_k
            else:
                dv[span] += more_v
                dk[span] += more_k
            qt += jnp.dot(keys_t[:, span], ds, preferred_element_type=F32)
        qt = qt * scale
        for i in range(GROUP):
            qg_ref[:, lanes(k * heads + p * GROUP + i, WIDTH)] = (
                qt[:, i * rows : (i + 1) * rows].T.astype(BF16)
            )

    def qg_copy(j):
        at = lanes(head_at(j), heads * WIDTH)
        return pltpu.make_async_copy(qg_ref.at[:, at], qg_hbm.at[:, at], qg_sem.at[j])

    def pair_copy(j):
        return remote(dpre.at[j, 1 - par], pair_in.at[j], pair_send.at[j], pair_recv.at[j], (partner, z))

    def plane_copy(j, other):
        to = lax.rem(half + other, halves)
        at = j * halves + other
        return remote(
            pair_sum.at[j, to], plane_in.at[j, other], plane_send.at[at], plane_recv.at[at],
            (2 * to + par, z),
        )

    def line_copy(j):
        return remote(
            plane_sum.at[j], line_in.at[j], line_send.at[j], line_recv.at[j], (me, head_at(j))
        )

    def dia_copy(j, b):
        k = head_at(j)
        return remote(
            ddia.at[j, b], dia_in.at[z, k], dia_send.at[j * tp_n + b], dia_recv.at[z * tp_n + k], (me, b)
        )

    def leave(j):
        for d in range(dp_n):
            at = slice(d * part, (d + 1) * part)
            dpre[j, d % 2, d // 2, 0] = (dk[at] * scale).astype(BF16)
            dpre[j, d % 2, d // 2, 1] = dv[at].astype(BF16)
        pair_copy(j).start()
        for b in range(tp_n):
            at = slice(pre + b * rows, pre + (b + 1) * rows)
            ddia[j, b, 0] = (dk[at] * scale).astype(BF16)
            ddia[j, b, 1] = dv[at].astype(BF16)
        for b in range(tp_n - 1):

            @pl.when(b < z)
            def _():
                dia_copy(j, b).start()

        qg_copy(j).start()

    def to_plane(j):
        pair_copy(j).wait_recv()
        for other in list(range(1, halves)) + [0]:
            to = lax.rem(half + other, halves)
            pair_sum[j, to] = (dpre[j, par, to].astype(F32) + pair_in[j, to].astype(F32)).astype(BF16)
            if other:
                plane_copy(j, other).start()

    def plane_total(j):
        acc = pair_sum[j, half].astype(F32)
        for other in range(1, halves):
            plane_copy(j, other).wait_recv()
            acc += plane_in[j, other].astype(F32)
        return acc

    def to_line(j):
        acc = plane_total(j)

        @pl.when(j == 0)
        def _():
            grad_ref[...] = acc

        @pl.when(j > 0)
        def _():
            plane_sum[j] = acc.astype(BF16)
            line_copy(j).start()

    @pl.loop(0, tp_n)
    def _(j):
        k = head_at(j)
        for other in range(halves):
            pre_await(k, 2 * lax.rem(half + other, halves) + 1 - par)
        for b in range(tp_n - 1):

            @pl.when(b < z)
            def _():
                at = gkv.at[k, b]
                remote(at, at, kv_send.at[0], kv_recv.at[k * tp_n + b], (partner, z)).wait_recv()

        pl.when(lax.rem(j, 2) == 0)(lambda: swap_all(k, j))
        pl.when((lax.rem(j, 2) == 0) & (j + 2 < tp_n))(lambda: kv_send_all(j + 2))
        keys[:pre] = gp[k, :, 0].reshape(pre, WIDTH)
        vals[:pre] = gp[k, :, 1].reshape(pre, WIDTH)
        keys[pre:] = gkv[k, :, 0].reshape(dia, WIDTH)
        vals[pre:] = gkv[k, :, 1].reshape(dia, WIDTH)
        for span in spans:
            keys_t[:, span] = keys[span].T

        attend(k, 0, lambda: pl.when(j > 0)(lambda: to_plane(j - 1)))
        pl.when(j + 1 < tp_n)(lambda: relay_all(head_at(j + 1), j + 1))
        pl.when(j + 2 < tp_n)(lambda: spread_all(j + 2))
        pl.when(j > 1)(lambda: to_line(j - 2))
        for p in range(1, steps):
            attend(k, p, lambda: None)
        leave(j)

    to_plane(tp_n - 1)
    if tp_n > 1:
        to_line(jnp.int32(tp_n - 2))
    to_line(jnp.int32(tp_n - 1))

    def own_dia(k):
        gray = flip(jnp.int32(k), z)
        j = gray
        for bit in range(1, bits):
            j = flip(j, gray // 2**bit)
        return ddia[j, z].astype(F32)

    for k in range(tp_n):
        dia_acc[k] = own_dia(k)
    for b in range(1, tp_n):

        @pl.when(z < b)
        def _():
            for k in range(tp_n):
                at = dia_in.at[b, k]
                remote(at, at, dia_send.at[0], dia_recv.at[b * tp_n + k], (partner, z)).wait_recv()
                dia_acc[k] += dia_in[b, k].astype(F32)

    for k in range(tp_n):
        at = slice(k * WIDTH, (k + 1) * WIDTH)
        kvg_ref[0, :, at] = dia_acc[k, 0].astype(BF16)
        kvg_ref[1, :, at] = dia_acc[k, 1].astype(BF16)

    for j in range(1, tp_n):
        remote(line_in.at[j], line_in.at[j], line_send.at[j], line_recv.at[j], (partner, z)).wait_recv()
        grad_ref[...] += line_in[j].astype(F32)

    @pl.loop(0, tp_n)
    def _(j):
        qg_copy(j).wait()
        pair_copy(j).wait_send()
        for other in range(halves):
            pre_spread(z, j, other).wait_send()
        for other in range(1, halves):
            plane_copy(j, other).wait_send()
            pre_relay(z, j, other).wait_send()
        for b in range(tp_n - 1):

            @pl.when(b < z)
            def _():
                dia_copy(j, b).wait_send()

        for other in range(1, tp_n):

            @pl.when((z + other < tp_n) & (lax.rem(j, 2) == 0))
            def _():
                kv_copy(j, other).wait_send()

        for b in range(tp_n - 1):

            @pl.when((b < mate) & (lax.rem(j, 2) == 0))
            def _():
                kv_swap(head_at(j), j, b).wait_send()

        @pl.when(j > 0)
        def _():
            pre_across(j).wait_send()
            line_copy(j).wait_send()


def update_kernel(
    grad_ref, kvg_ref, qg_in, c_ref, m_ref, v_ref, qg_out, kg_ref, vg_ref, nc_ref, nm_ref, nv_ref, sem
):
    out = pltpu.make_async_copy(qg_in, qg_out, sem.at[0])
    out.start()
    kg_ref[...] = kvg_ref[0]
    vg_ref[...] = kvg_ref[1]
    for w in range(2):
        grad = grad_ref[w]
        new_m = BETA_ONE * m_ref[:, w, :] + (1.0 - BETA_ONE) * grad
        new_v = BETA_TWO * v_ref[:, w, :] + (1.0 - BETA_TWO) * grad * grad
        update = new_m / (1.0 - BETA_ONE**STEP) / (jnp.sqrt(new_v / (1.0 - BETA_TWO**STEP)) + ADAM_EPS)
        nc_ref[:, w, :] = c_ref[:, w, :] - LEARN_RATE * update
        nm_ref[:, w, :] = new_m
        nv_ref[:, w, :] = new_v
    out.wait()


def shards(dp_n, tp_n, queries, dkeys, dvals, out_grad, lengths, cartridge, first, second):
    rows, features = queries.shape[1:]
    assert dkeys.shape[2] == WIDTH * tp_n and cartridge.shape[2] == WIDTH
    assert tp_n & (tp_n - 1) == 0
    part = cartridge.shape[0]
    pre = part * dp_n
    dia = rows * tp_n
    total = pre + dia
    halves = dp_n // 2
    scale = WIDTH ** (-0.5)
    sds = jax.ShapeDtypeStruct
    vm = pl.BlockSpec(memory_space=VMEM)
    hbm = pl.BlockSpec(memory_space=pl.ANY)
    dma = lambda n: pltpu.SemaphoreType.DMA((n,))
    block = (2, part, WIDTH)
    tile = (2, rows, WIDTH)
    wide = rows * GROUP

    grad, kvg, qg = pl.pallas_call(
        functools.partial(fused_kernel, dp_n, tp_n, scale),
        out_shape=(
            sds(block, F32), sds((2, rows, dkeys.shape[2]), BF16), sds((rows, features), BF16),
        ),
        in_specs=[pl.BlockSpec(memory_space=pltpu.SMEM), hbm, vm, vm, hbm, hbm],
        out_specs=(vm, vm, hbm),
        scratch_shapes=[
            VMEM((part, 2, WIDTH), F32), VMEM(block, BF16),
            VMEM((rows, features), BF16), VMEM((rows, features), BF16), VMEM((rows, features), BF16),
            VMEM((tp_n, dp_n) + block, BF16), VMEM((tp_n, tp_n) + tile, BF16),
            VMEM((total, WIDTH), BF16), VMEM((total, WIDTH), BF16), VMEM((WIDTH, total), BF16),
            VMEM((total, WIDTH), F32), VMEM((total, WIDTH), F32),
            VMEM((total, wide), F32), VMEM((total, wide), F32), VMEM((total, wide), F32),
            VMEM((tp_n, 2, halves) + block, BF16), VMEM((tp_n, tp_n) + tile, BF16),
            VMEM((tp_n, halves) + block, BF16), VMEM((tp_n, halves) + block, BF16),
            VMEM((tp_n, halves) + block, BF16), VMEM((tp_n,) + block, BF16), VMEM((tp_n,) + block, BF16),
            VMEM((tp_n, tp_n) + tile, BF16), VMEM((tp_n,) + tile, F32),
            dma(4), dma(2 * tp_n), dma(tp_n), dma(tp_n + tp_n * halves), dma(tp_n * dp_n),
            dma(tp_n * tp_n), dma(tp_n * tp_n), dma(tp_n * tp_n), dma(tp_n * halves),
            dma(tp_n), dma(tp_n), dma(tp_n * halves), dma(tp_n * halves), dma(tp_n), dma(tp_n),
            dma(tp_n * tp_n), dma(tp_n * tp_n),
        ],
        compiler_params=pltpu.CompilerParams(
            collective_id=0, has_side_effects=True, vmem_limit_bytes=56 * 2**20,
        ),
        name="fused",
    )(lengths, cartridge, dkeys[0], dvals[0], queries[0], out_grad[0])

    state = sds((part, 2, WIDTH), F32)
    qg, kg, vg, new_c, new_m, new_v = pl.pallas_call(
        update_kernel,
        out_shape=(
            sds((rows, features), BF16), sds((rows, dkeys.shape[2]), BF16), sds((rows, dkeys.shape[2]), BF16),
            state, state, state,
        ),
        in_specs=[vm] * 6,
        out_specs=(hbm,) + (vm,) * 5,
        scratch_shapes=[dma(1)],
        name="update",
    )(grad, kvg, qg, cartridge, first, second)
    return (qg[None], kg[None], vg[None], new_c, new_m, new_v)


def solution(mesh):
    tokens = P("dp", "tensor", None)
    prefix = P("dp", None, "tensor")
    return jax.shard_map(
        functools.partial(shards, mesh.shape["dp"], mesh.shape["tensor"]),
        mesh=mesh,
        in_specs=(tokens, tokens, tokens, tokens, P("dp"), prefix, prefix, prefix),
        out_specs=(tokens, tokens, tokens, prefix, prefix, prefix),
        check_vma=False,
    )
```

```python
import functools
import math

import jax
import jax.numpy as jnp
from jax import lax
from jax.experimental import pallas as pl
from jax.experimental.pallas import tpu as pltpu
from jax.sharding import PartitionSpec as P

STEP = 10
BETA_ONE = 0.9
BETA_TWO = 0.999
ADAM_EPS = 1e-08
LEARN_RATE = 0.01
MASKED = -1e30
WIDTH = 128
GROUP = 4
VMEM = pltpu.VMEM
MESH = pl.DeviceIdType.MESH
F32 = jnp.float32
BF16 = jnp.bfloat16


def greet(dp_n, tp_n, me, z):
    barrier = pltpu.get_barrier_semaphore()
    for other in range(1, tp_n):
        pl.semaphore_signal(
            barrier, inc=1, device_id=(me, lax.rem(z + other, tp_n)), device_id_type=MESH
        )
    half, par = me // 2, lax.rem(me, 2)
    pl.semaphore_signal(barrier, inc=1, device_id=(2 * half + 1 - par, z), device_id_type=MESH)
    for other in range(1, dp_n // 2):
        peer = 2 * lax.rem(half + other, dp_n // 2) + par
        pl.semaphore_signal(barrier, inc=1, device_id=(peer, z), device_id_type=MESH)
    return lambda: pl.semaphore_wait(barrier, tp_n - 1 + dp_n // 2)


def fused_kernel(
    dp_n, tp_n, scale, len_ref, cart_hbm, k_hbm, v_hbm, q_hbm, g_hbm, grad_ref, kvg_ref, qg_hbm,
    cart_ref, pre_ref, q_ref, g_ref, qg_ref, gp, gkv, keys, vals, keys_t, dk, dv, sc, ec, dc,
    dpre, ddia, pair_in, pair_sum, plane_in, plane_sum, line_in, dia_in, dia_near, dia_acc,
    local, kv_local, qg_sem, pre_send, pre_recv, kv_send, kv_recv, swap_send, relay,
    pair_send, pair_recv, plane_send, plane_recv, line_send, line_recv, dia_send, dia_recv, near_recv,
):
    me, z = lax.axis_index("dp"), lax.axis_index("tensor")
    half, par = me // 2, lax.rem(me, 2)
    halves = dp_n // 2
    partner = 2 * half + 1 - par
    rows = k_hbm.shape[0]
    total = keys.shape[0]
    dia = tp_n * rows
    pre = total - dia
    part = pre_ref.shape[1]
    heads = q_ref.shape[1] // WIDTH // tp_n
    steps = heads // GROUP
    wide = rows * GROUP
    chunk = 512
    spans = [slice(at, at + chunk) for at in range(0, total, chunk)]

    def remote(src, dst, s, r, to):
        return pltpu.make_async_remote_copy(
            src_ref=src, dst_ref=dst, send_sem=s, recv_sem=r, device_id=to, device_id_type=MESH
        )

    def lanes(k, width):
        return pl.ds(pl.multiple_of(k * width, width), width)

    arrive = greet(dp_n, tp_n, me, z)
    keep = [
        pltpu.make_async_copy(q_hbm, q_ref, local.at[0]),
        pltpu.make_async_copy(g_hbm, g_ref, local.at[1]),
    ] + [
        pltpu.make_async_copy(
            (k_hbm, v_hbm)[w].at[:, k * WIDTH : (k + 1) * WIDTH], gkv.at[k, z, w], kv_local.at[2 * k + w]
        )
        for k in range(tp_n)
        for w in range(2)
    ]
    cart_copy = pltpu.make_async_copy(cart_hbm, cart_ref, local.at[2])
    cart_copy.start()
    for copy in keep[2:] + keep[:2]:
        copy.start()
    cart_copy.wait()
    for w in range(2):
        pre_ref[w] = cart_ref[:, w, :].astype(BF16)
    own_copy = pltpu.make_async_copy(pre_ref, gp.at[z, me], local.at[3])
    own_copy.start()
    for copy in keep[2:]:
        copy.wait()
    keep = keep[:2] + [own_copy]
    arrive()

    bits = tp_n.bit_length() - 1

    def flip(a, b):
        out = 0
        for bit in range(bits):
            u, v = lax.rem(a // 2**bit, 2), lax.rem(b // 2**bit, 2)
            out = out + 2**bit * (u + v - 2 * u * v)
        return out

    def head_at(j):
        at = tp_n - 1 - jnp.int32(j)
        return flip(z, flip(at, at // 2))

    mate = z + 1 - 2 * lax.rem(z, 2)

    def leads(j):
        return (lax.rem(j, 2) == 0) & (j < tp_n - 1)

    def pre_across(j):
        return remote(
            pre_ref, gp.at[z, me], pre_send.at[j], pre_recv.at[z * dp_n + me], (me, head_at(j))
        )

    def pre_forward(t, j):
        return remote(gp.at[t, me], gp.at[t, me], pre_send.at[j + 1], pre_recv.at[t * dp_n + me], (me, mate))

    def pre_spread(t, j, other):
        to = 2 * lax.rem(half + other, halves) + par if other else partner
        return remote(
            gp.at[t, me], gp.at[t, me], pre_send.at[tp_n + j * halves + other], pre_recv.at[t * dp_n + me], (to, z)
        )

    def pre_relay(t, j, other):
        d = 2 * lax.rem(half + halves - other, halves) + par
        return remote(
            gp.at[t, d], gp.at[t, d], relay.at[j * halves + other], pre_recv.at[t * dp_n + d], (partner, z)
        )

    def pre_await(t, d):
        remote(gp.at[t, d], gp.at[t, d], pre_send.at[0], pre_recv.at[t * dp_n + d], (partner, z)).wait_recv()

    def kv_copy(j, other):
        at = tp_n - 1 - jnp.int32(j)
        k = flip(z + other, flip(at, at // 2))
        return remote(
            gkv.at[k, z], gkv.at[k, z], kv_send.at[other * tp_n + j], kv_recv.at[k * tp_n + z], (me, z + other)
        )

    def kv_swap(k, j, b):
        return remote(gkv.at[k, b], gkv.at[k, b], swap_send.at[j * tp_n + b], kv_recv.at[k * tp_n + b], (me, mate))

    def kv_send_all(j):
        for other in range(tp_n - 1, 0, -1):

            @pl.when(z + other < tp_n)
            def _():
                kv_copy(j, other).start()

    def swap_all(k, j):
        for b in range(tp_n - 1):

            @pl.when(b < mate)
            def _():
                kv_swap(k, j, b).start()

    for j in range(0, tp_n - 1, 2):
        pre_across(j).start()
        if j == 0:
            kv_send_all(j)

    for b in range(1, tp_n):

        @pl.when(z < b)
        def _():
            gkv[:, b] = jnp.zeros((tp_n, 2, rows, WIDTH), BF16)

    for copy in keep:
        copy.wait()

    def relay_all(t, j):
        for other in range(1, halves):
            copy = pre_relay(t, j, other)
            copy.wait_recv()
            copy.start()

    def spread_all(j):
        t = head_at(j)
        pl.when(j < tp_n - 1)(lambda: pre_await(t, me))
        pl.when(leads(j) & (j + 1 < tp_n - 1))(lambda: pre_forward(t, j).start())
        for other in list(range(1, halves)) + [0]:
            pre_spread(t, j, other).start()

    spread_all(jnp.int32(0))
    relay_all(head_at(0), 0)
    if tp_n > 1:
        spread_all(jnp.int32(1))

    real = z * rows + lax.broadcasted_iota(jnp.int32, (rows, WIDTH), 0) < len_ref[0]
    nt = (((1,), (1,)), ((), ()))
    fold = scale * math.log2(math.e)

    def attend(k, p, between):
        def cut(ref, i):
            return ref[:, lanes(k * heads + p * GROUP + i, WIDTH)]

        q = jnp.concatenate([cut(q_ref, i) for i in range(GROUP)], 0)
        g = jnp.concatenate(
            [jnp.where(real, cut(g_ref, i).astype(F32), 0.0).astype(BF16) for i in range(GROUP)], 0
        )
        top = jnp.full((1, wide), MASKED, F32)
        row_pos = z * rows + lax.rem(lax.broadcasted_iota(jnp.int32, (chunk, wide), 1), rows)
        lead = lax.broadcasted_iota(jnp.int32, (chunk, wide), 0) - row_pos
        for span in spans:
            s = lax.dot_general(keys[span], q, nt, preferred_element_type=F32)
            if span.start >= pre:
                s = jnp.where(lead <= pre - span.start, s, MASKED)
            sc[span] = s
            top = jnp.maximum(top, jnp.max(s, axis=0, keepdims=True))
        norm = jnp.zeros((1, wide), F32)
        mix = jnp.zeros((1, wide), F32)
        for span in spans:
            e = jnp.exp2((sc[span] - top) * fold)
            d = lax.dot_general(vals[span], g, nt, preferred_element_type=F32)
            norm += jnp.sum(e, axis=0, keepdims=True)
            mix += jnp.sum(e * d, axis=0, keepdims=True)
            ec[span] = e
            dc[span] = d
        inv = 1.0 / norm
        row_dot = mix * inv
        between()
        qt = jnp.zeros((WIDTH, wide), F32)
        for span in spans:
            w = ec[span] * inv
            ds = (w * (dc[span] - row_dot)).astype(BF16)
            more_v = jnp.dot(w.astype(BF16), g, preferred_element_type=F32)
            more_k = jnp.dot(ds, q, preferred_element_type=F32)
            if p == 0:
                dv[span] = more_v
                dk[span] = more_k
            else:
                dv[span] += more_v
                dk[span] += more_k
            qt += jnp.dot(keys_t[:, span], ds, preferred_element_type=F32)
        qt = qt * scale
        for i in range(GROUP):
            qg_ref[:, lanes(k * heads + p * GROUP + i, WIDTH)] = (
                qt[:, i * rows : (i + 1) * rows].T.astype(BF16)
            )

    def qg_copy(j):
        at = lanes(head_at(j), heads * WIDTH)
        return pltpu.make_async_copy(qg_ref.at[:, at], qg_hbm.at[:, at], qg_sem.at[j])

    def pair_copy(j):
        return remote(dpre.at[j, 1 - par], pair_in.at[j], pair_send.at[j], pair_recv.at[j], (partner, z))

    def plane_copy(j, other):
        to = lax.rem(half + other, halves)
        at = j * halves + other
        return remote(
            pair_sum.at[j, to], plane_in.at[j, other], plane_send.at[at], plane_recv.at[at],
            (2 * to + par, z),
        )

    def line_copy(j):
        return remote(
            plane_sum.at[j], line_in.at[j], line_send.at[j], line_recv.at[j],
            (me, jnp.where(leads(j), mate, head_at(j))),
        )

    def led_by(j):
        return j - 1

    def line_take(j):
        remote(line_in.at[j], line_in.at[j], line_send.at[j], line_recv.at[j], (partner, z)).wait_recv()
        return line_in[j].astype(F32)

    def dia_trade(j, b):
        return remote(
            ddia.at[j, b], dia_near.at[j, b], dia_send.at[j * tp_n + b], near_recv.at[j * tp_n + b], (me, mate)
        )

    def dia_copy(j, b):
        k = head_at(j)
        return remote(
            ddia.at[j, b], dia_in.at[z // 2, k], dia_send.at[j * tp_n + b], dia_recv.at[(z // 2) * tp_n + k], (me, b)
        )

    def leave(j):
        for b in range(tp_n):
            at = slice(pre + b * rows, pre + (b + 1) * rows)

            ddia[j, b, 0] = (dk[at] * scale).astype(BF16)
            ddia[j, b, 1] = dv[at].astype(BF16)
        for b in range(tp_n - 1):
            pl.when((b < z) & leads(j))(lambda: dia_trade(j, b).start())

        for d in range(dp_n):
            at = slice(d * part, (d + 1) * part)
            dpre[j, d % 2, d // 2, 0] = (dk[at] * scale).astype(BF16)
            dpre[j, d % 2, d // 2, 1] = dv[at].astype(BF16)
        pair_copy(j).start()
        qg_copy(j).start()

    def dia_join(j):
        for b in range(tp_n - 1):

            @pl.when(b < mate)
            def _():
                dia_trade(led_by(j), b).wait_recv()
                ddia[j, b] = (ddia[j, b].astype(F32) + dia_near[led_by(j), b].astype(F32)).astype(BF16)

            pl.when(b < z)(lambda: dia_copy(j, b).start())

    def to_plane(j):
        pair_copy(j).wait_recv()
        for other in list(range(1, halves)) + [0]:
            to = lax.rem(half + other, halves)
            pair_sum[j, to] = (dpre[j, par, to].astype(F32) + pair_in[j, to].astype(F32)).astype(BF16)
            if other:
                plane_copy(j, other).start()

    def plane_total(j):
        acc = pair_sum[j, half].astype(F32)
        for other in range(1, halves):
            plane_copy(j, other).wait_recv()
            acc += plane_in[j, other].astype(F32)
        return acc

    def to_line(j):
        acc = plane_total(j)

        @pl.when(leads(j))
        def _():
            plane_sum[j] = acc.astype(BF16)
            line_copy(j).start()

        @pl.when(jnp.logical_not(leads(j)) & (j < tp_n - 1))
        def _():
            plane_sum[j] = (acc + line_take(led_by(j))).astype(BF16)
            line_copy(j).start()

        @pl.when(j == tp_n - 1)
        def _():
            grad_ref[...] = acc + line_take(led_by(j)) if tp_n > 1 else acc

    @pl.loop(0, tp_n)
    def _(j):
        k = head_at(j)
        for other in range(halves):
            pre_await(k, 2 * lax.rem(half + other, halves) + 1 - par)
        for b in range(tp_n - 1):

            @pl.when(b < z)
            def _():
                at = gkv.at[k, b]
                remote(at, at, kv_send.at[0], kv_recv.at[k * tp_n + b], (partner, z)).wait_recv()

        pl.when(leads(j))(lambda: swap_all(k, j))
        pl.when(leads(j) & (j + 2 < tp_n - 1))(lambda: kv_send_all(j + 2))
        keys[:pre] = gp[k, :, 0].reshape(pre, WIDTH)
        vals[:pre] = gp[k, :, 1].reshape(pre, WIDTH)
        keys[pre:] = gkv[k, :, 0].reshape(dia, WIDTH)
        vals[pre:] = gkv[k, :, 1].reshape(dia, WIDTH)
        for span in spans:
            keys_t[:, span] = keys[span].T

        def passing():
            pl.when((j > 1) & (lax.rem(j, 2) == 0))(lambda: to_line(j - 2))
            pl.when(j > 0)(lambda: to_plane(j - 1))
            pl.when((j > 1) & (lax.rem(j, 2) == 0))(lambda: dia_join(j - 1))

        def relaying():
            pl.when(j + 1 < tp_n)(lambda: relay_all(head_at(j + 1), j + 1))

        attend(k, 0, passing)
        pl.when(j + 2 < tp_n)(lambda: spread_all(j + 2))
        pl.when((j > 1) & (lax.rem(j, 2) == 1))(lambda: to_line(j - 2))
        for p in range(1, steps):
            attend(k, p, relaying if p == 1 else lambda: None)
        leave(j)

    if tp_n > 1:
        dia_join(tp_n - 1)
    to_plane(tp_n - 1)
    if tp_n > 1:
        to_line(jnp.int32(tp_n - 2))
    to_line(jnp.int32(tp_n - 1))

    def own_dia(k):
        gray = flip(jnp.int32(k), z)
        j = gray
        for bit in range(1, bits):
            j = flip(j, gray // 2**bit)
        return ddia[tp_n - 1 - j, z].astype(F32)

    for k in range(tp_n):
        dia_acc[k] = own_dia(k)
    def dia_take(pair, k):
        at = dia_in.at[pair, k]
        remote(at, at, dia_send.at[0], dia_recv.at[pair * tp_n + k], (partner, z)).wait_recv()
        dia_acc[k] += dia_in[pair, k].astype(F32)

    @pl.when(z < mate)
    def _():
        for j in range(tp_n):
            k = head_at(j)
            pl.when(leads(j))(lambda: dia_take(z // 2, k))

    for pair in range(1, tp_n // 2):

        @pl.when(z // 2 < pair)
        def _():
            for k in range(tp_n):
                dia_take(pair, k)

    for k in range(tp_n):
        at = slice(k * WIDTH, (k + 1) * WIDTH)
        kvg_ref[0, :, at] = dia_acc[k, 0].astype(BF16)
        kvg_ref[1, :, at] = dia_acc[k, 1].astype(BF16)

    for j in range(1, tp_n - 1, 2):
        grad_ref[...] += line_take(j)

    @pl.loop(0, tp_n)
    def _(j):
        qg_copy(j).wait()
        pair_copy(j).wait_send()
        for other in range(halves):
            pre_spread(z, j, other).wait_send()
        for other in range(1, halves):
            plane_copy(j, other).wait_send()
            pre_relay(z, j, other).wait_send()
        for b in range(tp_n - 1):

            @pl.when(b < z)
            def _():
                dia_copy(j, b).wait_send()

        for other in range(1, tp_n):

            @pl.when((z + other < tp_n) & leads(j))
            def _():
                kv_copy(j, other).wait_send()

        for b in range(tp_n - 1):

            @pl.when((b < mate) & leads(j))
            def _():
                kv_swap(head_at(j), j, b).wait_send()

        @pl.when(leads(j))
        def _():
            pre_across(j).wait_send()

        @pl.when(leads(j) & (j + 1 < tp_n - 1))
        def _():
            pre_forward(z, j).wait_send()

        @pl.when(j < tp_n - 1)
        def _():
            line_copy(j).wait_send()


def update_kernel(
    grad_ref, kvg_ref, qg_in, c_ref, m_ref, v_ref, qg_out, kg_ref, vg_ref, nc_ref, nm_ref, nv_ref, sem
):
    out = pltpu.make_async_copy(qg_in, qg_out, sem.at[0])
    out.start()
    kg_ref[...] = kvg_ref[0]
    vg_ref[...] = kvg_ref[1]
    for w in range(2):
        grad = grad_ref[w]
        new_m = BETA_ONE * m_ref[:, w, :] + (1.0 - BETA_ONE) * grad
        new_v = BETA_TWO * v_ref[:, w, :] + (1.0 - BETA_TWO) * grad * grad
        update = new_m / (1.0 - BETA_ONE**STEP) / (jnp.sqrt(new_v / (1.0 - BETA_TWO**STEP)) + ADAM_EPS)
        nc_ref[:, w, :] = c_ref[:, w, :] - LEARN_RATE * update
        nm_ref[:, w, :] = new_m
        nv_ref[:, w, :] = new_v
    out.wait()


def shards(dp_n, tp_n, queries, dkeys, dvals, out_grad, lengths, cartridge, first, second):
    rows, features = queries.shape[1:]
    assert dkeys.shape[2] == WIDTH * tp_n and cartridge.shape[2] == WIDTH
    assert tp_n & (tp_n - 1) == 0
    part = cartridge.shape[0]
    pre = part * dp_n
    dia = rows * tp_n
    total = pre + dia
    halves = dp_n // 2
    scale = WIDTH ** (-0.5)
    sds = jax.ShapeDtypeStruct
    vm = pl.BlockSpec(memory_space=VMEM)
    hbm = pl.BlockSpec(memory_space=pl.ANY)
    dma = lambda n: pltpu.SemaphoreType.DMA((n,))
    block = (2, part, WIDTH)
    tile = (2, rows, WIDTH)
    wide = rows * GROUP

    grad, kvg, qg = pl.pallas_call(
        functools.partial(fused_kernel, dp_n, tp_n, scale),
        out_shape=(
            sds(block, F32), sds((2, rows, dkeys.shape[2]), BF16), sds((rows, features), BF16),
        ),
        in_specs=[pl.BlockSpec(memory_space=pltpu.SMEM)] + [pl.BlockSpec(memory_space=pltpu.HBM)] * 5,
        out_specs=(vm, vm, hbm),
        scratch_shapes=[
            VMEM((part, 2, WIDTH), F32), VMEM(block, BF16),
            VMEM((rows, features), BF16), VMEM((rows, features), BF16), VMEM((rows, features), BF16),
            VMEM((tp_n, dp_n) + block, BF16), VMEM((tp_n, tp_n) + tile, BF16),
            VMEM((total, WIDTH), BF16), VMEM((total, WIDTH), BF16), VMEM((WIDTH, total), BF16),
            VMEM((total, WIDTH), F32), VMEM((total, WIDTH), F32),
            VMEM((total, wide), F32), VMEM((total, wide), F32), VMEM((total, wide), F32),
            VMEM((tp_n, 2, halves) + block, BF16), VMEM((tp_n, tp_n) + tile, BF16),
            VMEM((tp_n, halves) + block, BF16), VMEM((tp_n, halves) + block, BF16),
            VMEM((tp_n, halves) + block, BF16), VMEM((tp_n,) + block, BF16), VMEM((tp_n,) + block, BF16),
            VMEM((tp_n, tp_n) + tile, BF16), VMEM((tp_n, tp_n) + tile, BF16), VMEM((tp_n,) + tile, F32),
            dma(4), dma(2 * tp_n), dma(tp_n), dma(tp_n + tp_n * halves), dma(tp_n * dp_n),
            dma(tp_n * tp_n), dma(tp_n * tp_n), dma(tp_n * tp_n), dma(tp_n * halves),
            dma(tp_n), dma(tp_n), dma(tp_n * halves), dma(tp_n * halves), dma(tp_n), dma(tp_n),
            dma(tp_n * tp_n), dma(tp_n * tp_n), dma(tp_n * tp_n),
        ],
        compiler_params=pltpu.CompilerParams(
            collective_id=0, has_side_effects=True, vmem_limit_bytes=40 * 2**20,
        ),
        name="fused",
    )(lengths, *[pltpu.with_memory_space_constraint(a, pltpu.HBM) for a in (cartridge, dkeys[0], dvals[0], queries[0], out_grad[0])])

    state = sds((part, 2, WIDTH), F32)
    qg, kg, vg, new_c, new_m, new_v = pl.pallas_call(
        update_kernel,
        out_shape=(
            sds((rows, features), BF16), sds((rows, dkeys.shape[2]), BF16), sds((rows, dkeys.shape[2]), BF16),
            state, state, state,
        ),
        in_specs=[vm] * 6,
        out_specs=(hbm,) + (vm,) * 5,
        scratch_shapes=[dma(1)],
        compiler_params=pltpu.CompilerParams(vmem_limit_bytes=8 * 2**20),
        name="update",
    )(grad, kvg, qg, cartridge, first, second)
    return (qg[None], kg[None], vg[None], new_c, new_m, new_v)


def solution(mesh):
    tokens = P("dp", "tensor", None)
    prefix = P("dp", None, "tensor")
    return jax.shard_map(
        functools.partial(shards, mesh.shape["dp"], mesh.shape["tensor"]),
        mesh=mesh,
        in_specs=(tokens, tokens, tokens, tokens, P("dp"), prefix, prefix, prefix),
        out_specs=(tokens, tokens, tokens, prefix, prefix, prefix),
        check_vma=False,
    )
```

```python
import functools
import math

import jax
import jax.numpy as jnp
from jax import lax
from jax.experimental import pallas as pl
from jax.experimental.pallas import tpu as pltpu
from jax.sharding import PartitionSpec as P

STEP = 10
BETA_ONE = 0.9
BETA_TWO = 0.999
ADAM_EPS = 1e-08
LEARN_RATE = 0.01
MASKED = -1e30
WIDTH = 128
GROUP = 4
VMEM = pltpu.VMEM
MESH = pl.DeviceIdType.MESH
F32 = jnp.float32
BF16 = jnp.bfloat16


def greet(dp_n, tp_n, me, z):
    barrier = pltpu.get_barrier_semaphore()
    for other in range(1, tp_n):
        pl.semaphore_signal(
            barrier, inc=1, device_id=(me, lax.rem(z + other, tp_n)), device_id_type=MESH
        )
    half, par = me // 2, lax.rem(me, 2)
    pl.semaphore_signal(barrier, inc=1, device_id=(2 * half + 1 - par, z), device_id_type=MESH)
    for other in range(1, dp_n // 2):
        peer = 2 * lax.rem(half + other, dp_n // 2) + par
        pl.semaphore_signal(barrier, inc=1, device_id=(peer, z), device_id_type=MESH)
    return lambda: pl.semaphore_wait(barrier, tp_n - 1 + dp_n // 2)


def fused_kernel(
    dp_n, tp_n, scale, len_ref, cart_hbm, k_hbm, v_hbm, q_hbm, g_hbm, grad_ref, kvg_ref, qg_hbm,
    cart_ref, pre_ref, q_ref, g_ref, qg_ref, gp, gkv, keys, vals, keys_t, dk, dv, sc0, ec0, dc0, sc1, ec1, dc1,
    dpre, ddia, pair_in, pair_sum, plane_in, plane_sum, line_in, dia_in, dia_near, dia_acc,
    local, kv_local, qg_sem, pre_send, pre_recv, kv_send, kv_recv, swap_send, relay,
    pair_send, pair_recv, plane_send, plane_recv, line_send, line_recv, dia_send, dia_recv, near_recv,
):
    sc, ec, dc = (sc0, sc1), (ec0, ec1), (dc0, dc1)
    me, z = lax.axis_index("dp"), lax.axis_index("tensor")
    half, par = me // 2, lax.rem(me, 2)
    halves = dp_n // 2
    partner = 2 * half + 1 - par
    rows = k_hbm.shape[0]
    total = keys.shape[0]
    dia = tp_n * rows
    pre = total - dia
    part = pre_ref.shape[1]
    heads = q_ref.shape[1] // WIDTH // tp_n
    assert heads == 2 * GROUP
    wide = rows * GROUP
    chunk = 512
    spans = [slice(at, at + chunk) for at in range(0, total, chunk)]

    def remote(src, dst, s, r, to):
        return pltpu.make_async_remote_copy(
            src_ref=src, dst_ref=dst, send_sem=s, recv_sem=r, device_id=to, device_id_type=MESH
        )

    def lanes(k, width):
        return pl.ds(pl.multiple_of(k * width, width), width)

    arrive = greet(dp_n, tp_n, me, z)
    keep = [
        pltpu.make_async_copy(q_hbm, q_ref, local.at[0]),
        pltpu.make_async_copy(g_hbm, g_ref, local.at[1]),
    ] + [
        pltpu.make_async_copy(
            (k_hbm, v_hbm)[w].at[:, k * WIDTH : (k + 1) * WIDTH], gkv.at[k, z, w], kv_local.at[2 * k + w]
        )
        for k in range(tp_n)
        for w in range(2)
    ]
    cart_copy = pltpu.make_async_copy(cart_hbm, cart_ref, local.at[2])
    cart_copy.start()
    for copy in keep[2:] + keep[:2]:
        copy.start()
    cart_copy.wait()
    for w in range(2):
        pre_ref[w] = cart_ref[:, w, :].astype(BF16)
    own_copy = pltpu.make_async_copy(pre_ref, gp.at[z, me], local.at[3])
    own_copy.start()
    for copy in keep[2:]:
        copy.wait()
    keep = keep[:2] + [own_copy]
    arrive()

    bits = tp_n.bit_length() - 1

    def flip(a, b):
        out = 0
        for bit in range(bits):
            u, v = lax.rem(a // 2**bit, 2), lax.rem(b // 2**bit, 2)
            out = out + 2**bit * (u + v - 2 * u * v)
        return out

    def head_at(j):
        at = tp_n - 1 - jnp.int32(j)
        return flip(z, flip(at, at // 2))

    mate = z + 1 - 2 * lax.rem(z, 2)

    def leads(j):
        return (lax.rem(j, 2) == 0) & (j < tp_n - 1)

    def pre_across(j):
        return remote(
            pre_ref, gp.at[z, me], pre_send.at[j], pre_recv.at[z * dp_n + me], (me, head_at(j))
        )

    def pre_forward(t, j):
        return remote(gp.at[t, me], gp.at[t, me], pre_send.at[j + 1], pre_recv.at[t * dp_n + me], (me, mate))

    def pre_spread(t, j, other):
        to = 2 * lax.rem(half + other, halves) + par if other else partner
        return remote(
            gp.at[t, me], gp.at[t, me], pre_send.at[tp_n + j * halves + other], pre_recv.at[t * dp_n + me], (to, z)
        )

    def pre_relay(t, j, other):
        d = 2 * lax.rem(half + halves - other, halves) + par
        return remote(
            gp.at[t, d], gp.at[t, d], relay.at[j * halves + other], pre_recv.at[t * dp_n + d], (partner, z)
        )

    def pre_await(t, d):
        remote(gp.at[t, d], gp.at[t, d], pre_send.at[0], pre_recv.at[t * dp_n + d], (partner, z)).wait_recv()

    def kv_copy(j, other):
        at = tp_n - 1 - jnp.int32(j)
        k = flip(z + other, flip(at, at // 2))
        return remote(
            gkv.at[k, z], gkv.at[k, z], kv_send.at[other * tp_n + j], kv_recv.at[k * tp_n + z], (me, z + other)
        )

    def kv_swap(k, j, b):
        return remote(gkv.at[k, b], gkv.at[k, b], swap_send.at[j * tp_n + b], kv_recv.at[k * tp_n + b], (me, mate))

    def kv_await(k):
        for b in range(tp_n - 1):

            @pl.when(b < z)
            def _():
                at = gkv.at[k, b]
                remote(at, at, kv_send.at[0], kv_recv.at[k * tp_n + b], (partner, z)).wait_recv()

    def kv_send_all(j):
        for other in range(tp_n - 1, 0, -1):

            @pl.when(z + other < tp_n)
            def _():
                kv_copy(j, other).start()

    def swap_all(k, j):
        for b in range(tp_n - 1):

            @pl.when(b < mate)
            def _():
                kv_swap(k, j, b).start()

    for j in range(0, tp_n - 1, 2):
        pre_across(j).start()
        if j == 0:
            pl.when(z > 0)(lambda: kv_send_all(0))

    for b in range(1, tp_n):

        @pl.when(z < b)
        def _():
            gkv[:, b] = jnp.zeros((tp_n, 2, rows, WIDTH), BF16)

    for copy in keep:
        copy.wait()
    real = z * rows + lax.broadcasted_iota(jnp.int32, (rows, WIDTH), 0) < len_ref[0]
    for at in range(0, g_ref.shape[1], WIDTH):
        at = slice(at, at + WIDTH)
        g_ref[:, at] = jnp.where(real, g_ref[:, at].astype(F32), 0.0).astype(BF16)

    def relay_all(t, j):
        for other in range(1, halves):
            copy = pre_relay(t, j, other)
            copy.wait_recv()
            copy.start()

    def spread_all(j):
        t = head_at(j)
        pl.when(j < tp_n - 1)(lambda: pre_await(t, me))
        pl.when(leads(j) & (j + 1 < tp_n - 1))(lambda: pre_forward(t, j).start())
        for other in list(range(1, halves)) + [0]:
            pre_spread(t, j, other).start()

    spread_all(jnp.int32(0))
    pl.when(z == 0)(lambda: kv_send_all(0))
    relay_all(head_at(0), 0)
    if tp_n > 1:
        spread_all(jnp.int32(1))

    nt = (((1,), (1,)), ((), ()))
    fold = scale * math.log2(math.e)
    row_pos = z * rows + lax.rem(lax.broadcasted_iota(jnp.int32, (chunk, wide), 1), rows)
    lead = lax.broadcasted_iota(jnp.int32, (chunk, wide), 0) - row_pos

    def take(ref, k, p):
        return jnp.concatenate([ref[:, lanes(k * heads + p * GROUP + i, WIDTH)] for i in range(GROUP)], 0)

    def score(p, span, q, top):
        s = lax.dot_general(keys[span], q, nt, preferred_element_type=F32)
        if span.start >= pre:
            s = jnp.where(lead <= pre - span.start, s, MASKED)
        sc[p][span] = s
        return jnp.maximum(top, jnp.max(s, axis=0, keepdims=True))

    def weigh(p, span, g, top, norm, mix):
        e = jnp.exp2((sc[p][span] - top) * fold)
        d = lax.dot_general(vals[span], g, nt, preferred_element_type=F32)
        ec[p][span] = e
        dc[p][span] = d
        return norm + jnp.sum(e, axis=0, keepdims=True), mix + jnp.sum(e * d, axis=0, keepdims=True)

    def grads(p, span, q, g, inv, row_dot, qt):
        w = ec[p][span] * inv
        ds = (w * (dc[p][span] - row_dot)).astype(BF16)
        more_v = jnp.dot(w.astype(BF16), g, preferred_element_type=F32)
        more_k = jnp.dot(ds, q, preferred_element_type=F32)
        if p == 0:
            dv[span] = more_v
            dk[span] = more_k
        else:
            dv[span] += more_v
            dk[span] += more_k
        return qt + jnp.dot(keys_t[:, span], ds, preferred_element_type=F32)

    def put(k, p, qt):
        qt = qt * scale
        for i in range(GROUP):
            qg_ref[:, lanes(k * heads + p * GROUP + i, WIDTH)] = (
                qt[:, i * rows : (i + 1) * rows].T.astype(BF16)
            )

    def attend(j, k):
        none = jnp.zeros((1, wide), F32)
        low = jnp.full((1, wide), MASKED, F32)
        q, g = [take(q_ref, k, p) for p in range(2)], [take(g_ref, k, p) for p in range(2)]
        top = [low, low]
        norm, mix = [none, none], [none, none]
        qt = [jnp.zeros((WIDTH, wide), F32)] * 2
        for span in spans:
            top[0] = score(0, span, q[0], top[0])
        for span in spans:
            norm[0], mix[0] = weigh(0, span, g[0], top[0], norm[0], mix[0])
            top[1] = score(1, span, q[1], top[1])
        inv = 1.0 / norm[0]
        row_dot = mix[0] * inv
        def kv_ahead():
            kv_await(head_at(j + 1))
            swap_all(head_at(j + 1), j + 1)

        pl.when(leads(j + 1) & (j > 0))(kv_ahead)
        pl.when((j > 1) & (lax.rem(j, 2) == 0))(lambda: to_line(j - 2))
        pl.when(j > 0)(lambda: to_plane(j - 1))
        pl.when(j + 2 < tp_n)(lambda: spread_all(j + 2))
        q, g = [take(q_ref, k, p) for p in range(2)], [take(g_ref, k, p) for p in range(2)]
        for span in spans[::-1]:
            norm[1], mix[1] = weigh(1, span, g[1], top[1], norm[1], mix[1])
            qt[0] = grads(0, span, q[0], g[0], inv, row_dot, qt[0])
        put(k, 0, qt[0])
        inv = 1.0 / norm[1]
        row_dot = mix[1] * inv
        pl.when((j > 1) & (lax.rem(j, 2) == 1))(lambda: to_line(j - 2))
        pl.when(j + 1 < tp_n)(lambda: relay_all(head_at(j + 1), j + 1))
        late = [span for span in spans if span.start >= pre]
        early = [span for span in spans if span.start < pre]
        for span in late:
            qt[1] = grads(1, span, q[1], g[1], inv, row_dot, qt[1])
        leave_dia(j)
        if tp_n > 1:
            pl.when((j == tp_n - 1) & (z > mate))(lambda: dia_join(tp_n - 1))
        for span in early:
            qt[1] = grads(1, span, q[1], g[1], inv, row_dot, qt[1])
        put(k, 1, qt[1])
        leave_pre(j)

    def qg_copy(j):
        at = lanes(head_at(j), heads * WIDTH)
        return pltpu.make_async_copy(qg_ref.at[:, at], qg_hbm.at[:, at], qg_sem.at[j])

    def pair_copy(j):
        return remote(dpre.at[j, 1 - par], pair_in.at[j], pair_send.at[j], pair_recv.at[j], (partner, z))

    def plane_copy(j, other):
        to = lax.rem(half + other, halves)
        at = j * halves + other
        return remote(
            pair_sum.at[j, to], plane_in.at[j, other], plane_send.at[at], plane_recv.at[at],
            (2 * to + par, z),
        )

    def line_copy(j):
        return remote(
            plane_sum.at[j], line_in.at[j], line_send.at[j], line_recv.at[j],
            (me, jnp.where(leads(j), mate, head_at(j))),
        )

    def led_by(j):
        return j - 1

    def line_take(j):
        remote(line_in.at[j], line_in.at[j], line_send.at[j], line_recv.at[j], (partner, z)).wait_recv()
        return line_in[j].astype(F32)

    def dia_trade(j, b):
        return remote(
            ddia.at[j, b], dia_near.at[b], dia_send.at[j * tp_n + b], near_recv.at[b], (me, mate)
        )

    def dia_copy(j, b):
        k = head_at(j)
        return remote(
            ddia.at[j, b], dia_in.at[z, k], dia_send.at[j * tp_n + b], dia_recv.at[z * tp_n + k], (me, b)
        )

    def leave_dia(j):
        for b in range(tp_n):
            at = slice(pre + b * rows, pre + (b + 1) * rows)
            ddia[j, b, 0] = (dk[at] * scale).astype(BF16)
            ddia[j, b, 1] = dv[at].astype(BF16)
        for b in range(tp_n - 1):
            pl.when((b < z) & (j == tp_n - 2))(lambda: dia_trade(j, b).start())
            pl.when((b < z) & (j < tp_n - 2))(lambda: dia_copy(j, b).start())

    def leave_pre(j):
        for d in range(dp_n):
            at = slice(d * part, (d + 1) * part)
            dpre[j, d % 2, d // 2, 0] = (dk[at] * scale).astype(BF16)
            dpre[j, d % 2, d // 2, 1] = dv[at].astype(BF16)
        pair_copy(j).start()
        qg_copy(j).start()

    def dia_join(j):
        for b in range(tp_n - 1):

            @pl.when(b < mate)
            def _():
                dia_trade(j - 1, b).wait_recv()
                ddia[j, b] = (ddia[j, b].astype(F32) + dia_near[b].astype(F32)).astype(BF16)

            pl.when(b < z)(lambda: dia_copy(j, b).start())

    def to_plane(j):
        pair_copy(j).wait_recv()
        for other in list(range(1, halves)) + [0]:
            to = lax.rem(half + other, halves)
            pair_sum[j, to] = (dpre[j, par, to].astype(F32) + pair_in[j, to].astype(F32)).astype(BF16)
            if other:
                plane_copy(j, other).start()

    def plane_total(j):
        acc = pair_sum[j, half].astype(F32)
        for other in range(1, halves):
            plane_copy(j, other).wait_recv()
            acc += plane_in[j, other].astype(F32)
        return acc

    def to_line(j):
        acc = plane_total(j)

        @pl.when(leads(j))
        def _():
            plane_sum[j] = acc.astype(BF16)
            line_copy(j).start()

        @pl.when(jnp.logical_not(leads(j)) & (j < tp_n - 1))
        def _():
            plane_sum[j] = (acc + line_take(led_by(j))).astype(BF16)
            line_copy(j).start()

        @pl.when(j == tp_n - 1)
        def _():
            grad_ref[...] = acc + line_take(led_by(j)) if tp_n > 1 else acc

    @pl.loop(0, tp_n)
    def _(j):
        k = head_at(j)
        for other in range(halves):
            pre_await(k, 2 * lax.rem(half + other, halves) + 1 - par)
        pl.when((j == 0) | (lax.rem(j, 2) == 1))(lambda: kv_await(k))
        pl.when(j == 0)(lambda: swap_all(k, j))
        pl.when(leads(j) & (j + 2 < tp_n - 1))(lambda: kv_send_all(j + 2))
        keys[:pre] = gp[k, :, 0].reshape(pre, WIDTH)
        vals[:pre] = gp[k, :, 1].reshape(pre, WIDTH)
        keys[pre:] = gkv[k, :, 0].reshape(dia, WIDTH)
        vals[pre:] = gkv[k, :, 1].reshape(dia, WIDTH)
        for span in spans:
            keys_t[:, span] = keys[span].T

        attend(j, k)

    to_plane(tp_n - 1)
    if tp_n > 1:
        to_line(jnp.int32(tp_n - 2))
    if tp_n > 1:
        pl.when(z < mate)(lambda: dia_join(tp_n - 1))
    to_line(jnp.int32(tp_n - 1))

    def own_dia(k):
        gray = flip(jnp.int32(k), z)
        j = gray
        for bit in range(1, bits):
            j = flip(j, gray // 2**bit)
        return ddia[tp_n - 1 - j, z].astype(F32)

    for k in range(tp_n):
        dia_acc[k] = own_dia(k)
    for b in range(1, tp_n):

        @pl.when(z < b)
        def _():
            for j in range(tp_n):
                if j != tp_n - 2:
                    k = flip(jnp.int32(b), flip(z, head_at(j)))
                    at = dia_in.at[b, k]
                    remote(at, at, dia_send.at[0], dia_recv.at[b * tp_n + k], (partner, z)).wait_recv()
                    dia_acc[k] += dia_in[b, k].astype(F32)

    for k in range(tp_n):
        at = slice(k * WIDTH, (k + 1) * WIDTH)
        kvg_ref[0, :, at] = dia_acc[k, 0].astype(BF16)
        kvg_ref[1, :, at] = dia_acc[k, 1].astype(BF16)

    for j in range(1, tp_n - 1, 2):
        grad_ref[...] += line_take(j)

    @pl.loop(0, tp_n)
    def _(j):
        qg_copy(j).wait()
        pair_copy(j).wait_send()
        for other in range(halves):
            pre_spread(z, j, other).wait_send()
        for other in range(1, halves):
            plane_copy(j, other).wait_send()
            pre_relay(z, j, other).wait_send()
        for b in range(tp_n - 1):

            @pl.when(b < z)
            def _():
                dia_copy(j, b).wait_send()

        for other in range(1, tp_n):

            @pl.when((z + other < tp_n) & leads(j))
            def _():
                kv_copy(j, other).wait_send()

        for b in range(tp_n - 1):

            @pl.when((b < mate) & leads(j))
            def _():
                kv_swap(head_at(j), j, b).wait_send()

        @pl.when(leads(j))
        def _():
            pre_across(j).wait_send()

        @pl.when(leads(j) & (j + 1 < tp_n - 1))
        def _():
            pre_forward(z, j).wait_send()

        @pl.when(j < tp_n - 1)
        def _():
            line_copy(j).wait_send()


def update_kernel(
    grad_ref, kvg_ref, qg_in, c_ref, m_ref, v_ref, qg_out, kg_ref, vg_ref, nc_ref, nm_ref, nv_ref, sem
):
    out = pltpu.make_async_copy(qg_in, qg_out, sem.at[0])
    out.start()
    kg_ref[...] = kvg_ref[0]
    vg_ref[...] = kvg_ref[1]
    for w in range(2):
        grad = grad_ref[w]
        new_m = BETA_ONE * m_ref[:, w, :] + (1.0 - BETA_ONE) * grad
        new_v = BETA_TWO * v_ref[:, w, :] + (1.0 - BETA_TWO) * grad * grad
        update = new_m / (1.0 - BETA_ONE**STEP) / (jnp.sqrt(new_v / (1.0 - BETA_TWO**STEP)) + ADAM_EPS)
        nc_ref[:, w, :] = c_ref[:, w, :] - LEARN_RATE * update
        nm_ref[:, w, :] = new_m
        nv_ref[:, w, :] = new_v
    out.wait()


def shards(dp_n, tp_n, queries, dkeys, dvals, out_grad, lengths, cartridge, first, second):
    rows, features = queries.shape[1:]
    assert dkeys.shape[2] == WIDTH * tp_n and cartridge.shape[2] == WIDTH
    assert tp_n & (tp_n - 1) == 0
    part = cartridge.shape[0]
    pre = part * dp_n
    dia = rows * tp_n
    total = pre + dia
    halves = dp_n // 2
    scale = WIDTH ** (-0.5)
    sds = jax.ShapeDtypeStruct
    vm = pl.BlockSpec(memory_space=VMEM)
    hbm = pl.BlockSpec(memory_space=pl.ANY)
    dma = lambda n: pltpu.SemaphoreType.DMA((n,))
    block = (2, part, WIDTH)
    tile = (2, rows, WIDTH)
    wide = rows * GROUP

    grad, kvg, qg = pl.pallas_call(
        functools.partial(fused_kernel, dp_n, tp_n, scale),
        out_shape=(
            sds(block, F32), sds((2, rows, dkeys.shape[2]), BF16), sds((rows, features), BF16),
        ),
        in_specs=[pl.BlockSpec(memory_space=pltpu.SMEM)] + [pl.BlockSpec(memory_space=pltpu.HBM)] * 5,
        out_specs=(vm, vm, hbm),
        scratch_shapes=[
            VMEM((part, 2, WIDTH), F32), VMEM(block, BF16),
            VMEM((rows, features), BF16), VMEM((rows, features), BF16), VMEM((rows, features), BF16),
            VMEM((tp_n, dp_n) + block, BF16), VMEM((tp_n, tp_n) + tile, BF16),
            VMEM((total, WIDTH), BF16), VMEM((total, WIDTH), BF16), VMEM((WIDTH, total), BF16),
            VMEM((total, WIDTH), F32), VMEM((total, WIDTH), F32),
            *[VMEM((total, wide), F32)] * 6,
            VMEM((tp_n, 2, halves) + block, BF16), VMEM((tp_n, tp_n) + tile, BF16),
            VMEM((tp_n, halves) + block, BF16), VMEM((tp_n, halves) + block, BF16),
            VMEM((tp_n, halves) + block, BF16), VMEM((tp_n,) + block, BF16), VMEM((tp_n,) + block, BF16),
            VMEM((tp_n, tp_n) + tile, BF16), VMEM((tp_n,) + tile, BF16), VMEM((tp_n,) + tile, F32),
            dma(4), dma(2 * tp_n), dma(tp_n), dma(tp_n + tp_n * halves), dma(tp_n * dp_n),
            dma(tp_n * tp_n), dma(tp_n * tp_n), dma(tp_n * tp_n), dma(tp_n * halves),
            dma(tp_n), dma(tp_n), dma(tp_n * halves), dma(tp_n * halves), dma(tp_n), dma(tp_n),
            dma(tp_n * tp_n), dma(tp_n * tp_n), dma(tp_n),
        ],
        compiler_params=pltpu.CompilerParams(
            collective_id=0, has_side_effects=True, vmem_limit_bytes=40 * 2**20,
        ),
        name="fused",
    )(lengths, *[pltpu.with_memory_space_constraint(a, pltpu.HBM) for a in (cartridge, dkeys[0], dvals[0], queries[0], out_grad[0])])

    state = sds((part, 2, WIDTH), F32)
    qg, kg, vg, new_c, new_m, new_v = pl.pallas_call(
        update_kernel,
        out_shape=(
            sds((rows, features), BF16), sds((rows, dkeys.shape[2]), BF16), sds((rows, dkeys.shape[2]), BF16),
            state, state, state,
        ),
        in_specs=[vm] * 6,
        out_specs=(hbm,) + (vm,) * 5,
        scratch_shapes=[dma(1)],
        compiler_params=pltpu.CompilerParams(vmem_limit_bytes=8 * 2**20),
        name="update",
    )(grad, kvg, qg, cartridge, first, second)
    return (qg[None], kg[None], vg[None], new_c, new_m, new_v)


def solution(mesh):
    tokens = P("dp", "tensor", None)
    prefix = P("dp", None, "tensor")
    return jax.shard_map(
        functools.partial(shards, mesh.shape["dp"], mesh.shape["tensor"]),
        mesh=mesh,
        in_specs=(tokens, tokens, tokens, tokens, P("dp"), prefix, prefix, prefix),
        out_specs=(tokens, tokens, tokens, prefix, prefix, prefix),
        check_vma=False,
    )
```

```python
import functools
import math

import jax
import jax.numpy as jnp
from jax import lax
from jax.experimental import pallas as pl
from jax.experimental.pallas import tpu as pltpu
from jax.sharding import PartitionSpec as P

STEP = 10
BETA_ONE = 0.9
BETA_TWO = 0.999
ADAM_EPS = 1e-08
LEARN_RATE = 0.01
MASKED = -1e30
WIDTH = 128
GROUP = 4
VMEM = pltpu.VMEM
MESH = pl.DeviceIdType.MESH
F32 = jnp.float32
BF16 = jnp.bfloat16


def greet(dp_n, tp_n, me, z):
    barrier = pltpu.get_barrier_semaphore()
    for other in range(1, tp_n):
        pl.semaphore_signal(
            barrier, inc=1, device_id=(me, lax.rem(z + other, tp_n)), device_id_type=MESH
        )
    half, par = me // 2, lax.rem(me, 2)
    pl.semaphore_signal(barrier, inc=1, device_id=(2 * half + 1 - par, z), device_id_type=MESH)
    for other in range(1, dp_n // 2):
        peer = 2 * lax.rem(half + other, dp_n // 2) + par
        pl.semaphore_signal(barrier, inc=1, device_id=(peer, z), device_id_type=MESH)
    return lambda: pl.semaphore_wait(barrier, tp_n - 1 + dp_n // 2)


def fused_kernel(
    dp_n, tp_n, scale, len_ref, cart_hbm, k_hbm, v_hbm, q_hbm, g_hbm, grad_ref, kvg_ref, qg_hbm,
    cart_ref, pre_ref, q_ref, g_ref, qg_ref, gp, gkv, keys_t, dk, dv, sc0, ec0, dc0, sc1, ec1, dc1,
    dpre, ddia, pair_in, pair_sum, plane_in, plane_sum, line_in, dia_in, dia_near, dia_acc,
    local, kv_local, qg_sem, pre_send, pre_recv, kv_send, kv_recv, swap_send, relay,
    pair_send, pair_recv, plane_send, plane_recv, line_send, line_recv, dia_send, dia_recv, near_recv,
):
    sc, ec, dc = (sc0, sc1), (ec0, ec1), (dc0, dc1)
    me, z = lax.axis_index("dp"), lax.axis_index("tensor")
    half, par = me // 2, lax.rem(me, 2)
    halves = dp_n // 2
    partner = 2 * half + 1 - par
    rows = k_hbm.shape[0]
    total = keys_t.shape[1]
    dia = tp_n * rows
    pre = total - dia
    part = pre_ref.shape[1]
    heads = q_ref.shape[1] // WIDTH // tp_n
    assert heads == 2 * GROUP
    wide = rows * GROUP
    chunk = 512
    assert pre % chunk == 0 and chunk % rows == 0 and chunk % pre_ref.shape[1] == 0
    spans = [slice(at, at + chunk) for at in range(0, total, chunk)]

    def remote(src, dst, s, r, to):
        return pltpu.make_async_remote_copy(
            src_ref=src, dst_ref=dst, send_sem=s, recv_sem=r, device_id=to, device_id_type=MESH
        )

    def lanes(k, width):
        return pl.ds(pl.multiple_of(k * width, width), width)

    arrive = greet(dp_n, tp_n, me, z)
    keep = [
        pltpu.make_async_copy(q_hbm, q_ref, local.at[0]),
        pltpu.make_async_copy(g_hbm, g_ref, local.at[1]),
    ] + [
        pltpu.make_async_copy(
            (k_hbm, v_hbm)[w].at[:, k * WIDTH : (k + 1) * WIDTH], gkv.at[k, z, w], kv_local.at[2 * k + w]
        )
        for k in range(tp_n)
        for w in range(2)
    ]
    cart_copy = pltpu.make_async_copy(cart_hbm, cart_ref, local.at[2])
    cart_copy.start()
    for copy in keep[2:] + keep[:2]:
        copy.start()
    cart_copy.wait()
    for w in range(2):
        pre_ref[w] = cart_ref[:, w, :].astype(BF16)
    own_copy = pltpu.make_async_copy(pre_ref, gp.at[z, me], local.at[3])
    own_copy.start()
    for copy in keep[2:]:
        copy.wait()
    keep = keep[:2] + [own_copy]
    arrive()

    bits = tp_n.bit_length() - 1

    def flip(a, b):
        out = 0
        for bit in range(bits):
            u, v = lax.rem(a // 2**bit, 2), lax.rem(b // 2**bit, 2)
            out = out + 2**bit * (u + v - 2 * u * v)
        return out

    def head_at(j):
        at = tp_n - 1 - jnp.int32(j)
        return flip(z, flip(at, at // 2))

    mate = z + 1 - 2 * lax.rem(z, 2)

    def leads(j):
        return (lax.rem(j, 2) == 0) & (j < tp_n - 1)

    def pre_across(j):
        return remote(
            pre_ref, gp.at[z, me], pre_send.at[j], pre_recv.at[z * dp_n + me], (me, head_at(j))
        )

    def pre_forward(t, j):
        return remote(gp.at[t, me], gp.at[t, me], pre_send.at[j + 1], pre_recv.at[t * dp_n + me], (me, mate))

    def pre_spread(t, j, other):
        to = 2 * lax.rem(half + other, halves) + par if other else partner
        return remote(
            gp.at[t, me], gp.at[t, me], pre_send.at[tp_n + j * halves + other], pre_recv.at[t * dp_n + me], (to, z)
        )

    def pre_relay(t, j, other):
        d = 2 * lax.rem(half + halves - other, halves) + par
        return remote(
            gp.at[t, d], gp.at[t, d], relay.at[j * halves + other], pre_recv.at[t * dp_n + d], (partner, z)
        )

    def pre_await(t, d):
        remote(gp.at[t, d], gp.at[t, d], pre_send.at[0], pre_recv.at[t * dp_n + d], (partner, z)).wait_recv()

    def kv_copy(j, other):
        at = tp_n - 1 - jnp.int32(j)
        k = flip(z + other, flip(at, at // 2))
        return remote(
            gkv.at[k, z], gkv.at[k, z], kv_send.at[other * tp_n + j], kv_recv.at[k * tp_n + z], (me, z + other)
        )

    def kv_swap(k, j, b):
        return remote(gkv.at[k, b], gkv.at[k, b], swap_send.at[j * tp_n + b], kv_recv.at[k * tp_n + b], (me, mate))

    def kv_await(k):
        for b in range(tp_n - 1):

            @pl.when(b < z)
            def _():
                at = gkv.at[k, b]
                remote(at, at, kv_send.at[0], kv_recv.at[k * tp_n + b], (partner, z)).wait_recv()

    def kv_send_all(j):
        for other in range(tp_n - 1, 0, -1):

            @pl.when(z + other < tp_n)
            def _():
                kv_copy(j, other).start()

    def swap_all(k, j):
        for b in range(tp_n - 1):

            @pl.when(b < mate)
            def _():
                kv_swap(k, j, b).start()

    for j in range(0, tp_n - 1, 2):
        pre_across(j).start()
        if j == 0:
            pl.when(z > 0)(lambda: kv_send_all(0))

    for b in range(1, tp_n):

        @pl.when(z < b)
        def _():
            gkv[:, b] = jnp.zeros((tp_n, 2, rows, WIDTH), BF16)

    for copy in keep:
        copy.wait()
    real = z * rows + lax.broadcasted_iota(jnp.int32, (rows, WIDTH), 0) < len_ref[0]
    for at in range(0, g_ref.shape[1], WIDTH):
        at = slice(at, at + WIDTH)
        g_ref[:, at] = jnp.where(real, g_ref[:, at].astype(F32), 0.0).astype(BF16)

    def relay_all(t, j):
        for other in range(1, halves):
            copy = pre_relay(t, j, other)
            copy.wait_recv()
            copy.start()

    def spread_all(j):
        t = head_at(j)
        pl.when(j < tp_n - 1)(lambda: pre_await(t, me))
        pl.when(leads(j) & (j + 1 < tp_n - 1))(lambda: pre_forward(t, j).start())
        for other in list(range(1, halves)) + [0]:
            pre_spread(t, j, other).start()

    spread_all(jnp.int32(0))
    pl.when(z == 0)(lambda: kv_send_all(0))
    relay_all(head_at(0), 0)
    if tp_n > 1:
        spread_all(jnp.int32(1))

    nt = (((1,), (1,)), ((), ()))
    fold = scale * math.log2(math.e)
    row_pos = z * rows + lax.rem(lax.broadcasted_iota(jnp.int32, (chunk, wide), 1), rows)
    lead = lax.broadcasted_iota(jnp.int32, (chunk, wide), 0) - row_pos

    def take(ref, k, p):
        return jnp.concatenate([ref[:, lanes(k * heads + p * GROUP + i, WIDTH)] for i in range(GROUP)], 0)

    def rows_of(k, w, span):
        if span.start < pre:
            return gp[k, span.start // part : span.stop // part, w].reshape(chunk, WIDTH)
        at = slice((span.start - pre) // rows, (span.stop - pre) // rows)
        return gkv[k, at, w].reshape(chunk, WIDTH)

    def score(k, p, span, q, top):
        s = lax.dot_general(rows_of(k, 0, span), q, nt, preferred_element_type=F32)
        if span.start >= pre:
            s = jnp.where(lead <= pre - span.start, s, MASKED)
        sc[p][span] = s
        return jnp.maximum(top, jnp.max(s, axis=0, keepdims=True))

    def weigh(k, p, span, g, top, norm, mix):
        e = jnp.exp2((sc[p][span] - top) * fold)
        d = lax.dot_general(rows_of(k, 1, span), g, nt, preferred_element_type=F32)
        ec[p][span] = e
        dc[p][span] = d
        return norm + jnp.sum(e, axis=0, keepdims=True), mix + jnp.sum(e * d, axis=0, keepdims=True)

    def grads(p, span, q, g, inv, row_dot, qt):
        w = ec[p][span] * inv
        ds = (w * (dc[p][span] - row_dot)).astype(BF16)
        more_v = jnp.dot(w.astype(BF16), g, preferred_element_type=F32)
        more_k = jnp.dot(ds, q, preferred_element_type=F32)
        if p == 0:
            dv[span] = more_v
            dk[span] = more_k
        else:
            dv[span] += more_v
            dk[span] += more_k
        return qt + jnp.dot(keys_t[:, span], ds, preferred_element_type=F32)

    def put(k, p, qt):
        qt = qt * scale
        for i in range(GROUP):
            qg_ref[:, lanes(k * heads + p * GROUP + i, WIDTH)] = (
                qt[:, i * rows : (i + 1) * rows].T.astype(BF16)
            )

    def attend(j, k):
        none = jnp.zeros((1, wide), F32)
        low = jnp.full((1, wide), MASKED, F32)
        q, g = [take(q_ref, k, p) for p in range(2)], [take(g_ref, k, p) for p in range(2)]
        top = [low, low]
        norm, mix = [none, none], [none, none]
        qt = [jnp.zeros((WIDTH, wide), F32)] * 2
        for span in spans:
            top[0] = score(k, 0, span, q[0], top[0])
        for span in spans:
            norm[0], mix[0] = weigh(k, 0, span, g[0], top[0], norm[0], mix[0])
            top[1] = score(k, 1, span, q[1], top[1])
        inv = 1.0 / norm[0]
        row_dot = mix[0] * inv
        def kv_ahead():
            kv_await(head_at(j + 1))
            swap_all(head_at(j + 1), j + 1)

        pl.when(leads(j + 1) & (j > 0))(kv_ahead)
        pl.when(j > 1)(lambda: to_line(j - 2))
        pl.when(j > 0)(lambda: to_plane(j - 1))
        pl.when(j + 2 < tp_n)(lambda: spread_all(j + 2))
        q, g = [take(q_ref, k, p) for p in range(2)], [take(g_ref, k, p) for p in range(2)]
        for span in spans[::-1]:
            norm[1], mix[1] = weigh(k, 1, span, g[1], top[1], norm[1], mix[1])
            qt[0] = grads(0, span, q[0], g[0], inv, row_dot, qt[0])
        put(k, 0, qt[0])
        inv = 1.0 / norm[1]
        row_dot = mix[1] * inv
        late = [span for span in spans if span.start >= pre]
        early = [span for span in spans if span.start < pre]
        for span in late:
            qt[1] = grads(1, span, q[1], g[1], inv, row_dot, qt[1])
        pl.when(j + 1 < tp_n)(lambda: relay_all(head_at(j + 1), j + 1))
        leave_dia(j)
        if tp_n > 1:
            pl.when((j == tp_n - 1) & (z > mate))(lambda: dia_join(tp_n - 1))
        for span in early:
            qt[1] = grads(1, span, q[1], g[1], inv, row_dot, qt[1])
        put(k, 1, qt[1])
        leave_pre(j)

    def qg_copy(j):
        at = lanes(head_at(j), heads * WIDTH)
        return pltpu.make_async_copy(qg_ref.at[:, at], qg_hbm.at[:, at], qg_sem.at[j])

    def pair_copy(j):
        return remote(dpre.at[j, 1 - par], pair_in.at[j], pair_send.at[j], pair_recv.at[j], (partner, z))

    def plane_copy(j, other):
        to = lax.rem(half + other, halves)
        at = j * halves + other
        return remote(
            pair_sum.at[j, to], plane_in.at[j, other], plane_send.at[at], plane_recv.at[at],
            (2 * to + par, z),
        )

    def line_copy(j):
        return remote(
            plane_sum.at[j], line_in.at[j], line_send.at[j], line_recv.at[j],
            (me, jnp.where(leads(j), mate, head_at(j))),
        )

    def led_by(j):
        return j - 1

    def line_take(j):
        remote(line_in.at[j], line_in.at[j], line_send.at[j], line_recv.at[j], (partner, z)).wait_recv()
        return line_in[j].astype(F32)

    def dia_trade(j, b):
        return remote(
            ddia.at[j, b], dia_near.at[b], dia_send.at[j * tp_n + b], near_recv.at[b], (me, mate)
        )

    def dia_copy(j, b):
        k = head_at(j)
        return remote(
            ddia.at[j, b], dia_in.at[z, k], dia_send.at[j * tp_n + b], dia_recv.at[z * tp_n + k], (me, b)
        )

    def leave_dia(j):
        for b in range(tp_n):
            at = slice(pre + b * rows, pre + (b + 1) * rows)
            ddia[j, b, 0] = (dk[at] * scale).astype(BF16)
            ddia[j, b, 1] = dv[at].astype(BF16)
        for b in range(tp_n - 1):
            pl.when((b < z) & (j == tp_n - 2))(lambda: dia_trade(j, b).start())
            pl.when((b < z) & (j < tp_n - 2))(lambda: dia_copy(j, b).start())

    def leave_pre(j):
        for d in range(dp_n):
            at = slice(d * part, (d + 1) * part)
            dpre[j, d % 2, d // 2, 0] = (dk[at] * scale).astype(BF16)
            dpre[j, d % 2, d // 2, 1] = dv[at].astype(BF16)
        pair_copy(j).start()
        qg_copy(j).start()

    def dia_join(j):
        for b in range(tp_n - 1):

            @pl.when(b < mate)
            def _():
                dia_trade(j - 1, b).wait_recv()
                ddia[j, b] = (ddia[j, b].astype(F32) + dia_near[b].astype(F32)).astype(BF16)

            pl.when(b < z)(lambda: dia_copy(j, b).start())

    def to_plane(j):
        pair_copy(j).wait_recv()
        for other in list(range(1, halves)) + [0]:
            to = lax.rem(half + other, halves)
            pair_sum[j, to] = (dpre[j, par, to].astype(F32) + pair_in[j, to].astype(F32)).astype(BF16)
            if other:
                plane_copy(j, other).start()

    def plane_total(j):
        acc = pair_sum[j, half].astype(F32)
        for other in range(1, halves):
            plane_copy(j, other).wait_recv()
            acc += plane_in[j, other].astype(F32)
        return acc

    def to_line(j):
        acc = plane_total(j)

        @pl.when(leads(j))
        def _():
            plane_sum[j] = acc.astype(BF16)
            line_copy(j).start()

        @pl.when(jnp.logical_not(leads(j)) & (j < tp_n - 1))
        def _():
            plane_sum[j] = (acc + line_take(led_by(j))).astype(BF16)
            line_copy(j).start()

        @pl.when(j == tp_n - 1)
        def _():
            grad_ref[...] = acc + line_take(led_by(j)) if tp_n > 1 else acc

    @pl.loop(0, tp_n)
    def _(j):
        k = head_at(j)
        for other in range(halves):
            pre_await(k, 2 * lax.rem(half + other, halves) + 1 - par)
        pl.when((j == 0) | (lax.rem(j, 2) == 1))(lambda: kv_await(k))
        pl.when(j == 0)(lambda: swap_all(k, j))
        pl.when(leads(j) & (j + 2 < tp_n - 1))(lambda: kv_send_all(j + 2))
        for span in spans:
            keys_t[:, span] = rows_of(k, 0, span).T

        attend(j, k)

    to_plane(tp_n - 1)
    if tp_n > 1:
        to_line(jnp.int32(tp_n - 2))
    if tp_n > 1:
        pl.when(z < mate)(lambda: dia_join(tp_n - 1))
    to_line(jnp.int32(tp_n - 1))

    def own_dia(k):
        gray = flip(jnp.int32(k), z)
        j = gray
        for bit in range(1, bits):
            j = flip(j, gray // 2**bit)
        return ddia[tp_n - 1 - j, z].astype(F32)

    for k in range(tp_n):
        dia_acc[k] = own_dia(k)
    for b in range(1, tp_n):

        @pl.when(z < b)
        def _():
            for j in range(tp_n):
                if j != tp_n - 2:
                    k = flip(jnp.int32(b), flip(z, head_at(j)))
                    at = dia_in.at[b, k]
                    remote(at, at, dia_send.at[0], dia_recv.at[b * tp_n + k], (partner, z)).wait_recv()
                    dia_acc[k] += dia_in[b, k].astype(F32)

    for k in range(tp_n):
        at = slice(k * WIDTH, (k + 1) * WIDTH)
        kvg_ref[0, :, at] = dia_acc[k, 0].astype(BF16)
        kvg_ref[1, :, at] = dia_acc[k, 1].astype(BF16)

    for j in range(1, tp_n - 1, 2):
        grad_ref[...] += line_take(j)

    @pl.loop(0, tp_n)
    def _(j):
        qg_copy(j).wait()
        pair_copy(j).wait_send()
        for other in range(halves):
            pre_spread(z, j, other).wait_send()
        for other in range(1, halves):
            plane_copy(j, other).wait_send()
            pre_relay(z, j, other).wait_send()
        for b in range(tp_n - 1):

            @pl.when(b < z)
            def _():
                dia_copy(j, b).wait_send()

        for other in range(1, tp_n):

            @pl.when((z + other < tp_n) & leads(j))
            def _():
                kv_copy(j, other).wait_send()

        for b in range(tp_n - 1):

            @pl.when((b < mate) & leads(j))
            def _():
                kv_swap(head_at(j), j, b).wait_send()

        @pl.when(leads(j))
        def _():
            pre_across(j).wait_send()

        @pl.when(leads(j) & (j + 1 < tp_n - 1))
        def _():
            pre_forward(z, j).wait_send()

        @pl.when(j < tp_n - 1)
        def _():
            line_copy(j).wait_send()


def update_kernel(
    grad_ref, kvg_ref, qg_in, c_ref, m_ref, v_ref, qg_out, kg_ref, vg_ref, nc_ref, nm_ref, nv_ref, sem
):
    out = pltpu.make_async_copy(qg_in, qg_out, sem.at[0])
    out.start()
    halves = [pltpu.make_async_copy(kvg_ref.at[w], (kg_ref, vg_ref)[w], sem.at[1 + w]) for w in range(2)]
    for copy in halves:
        copy.start()
    for w in range(2):
        grad = grad_ref[w]
        new_m = BETA_ONE * m_ref[:, w, :] + (1.0 - BETA_ONE) * grad
        new_v = BETA_TWO * v_ref[:, w, :] + (1.0 - BETA_TWO) * grad * grad
        update = new_m / (1.0 - BETA_ONE**STEP) / (jnp.sqrt(new_v / (1.0 - BETA_TWO**STEP)) + ADAM_EPS)
        nc_ref[:, w, :] = c_ref[:, w, :] - LEARN_RATE * update
        nm_ref[:, w, :] = new_m
        nv_ref[:, w, :] = new_v
    for copy in halves + [out]:
        copy.wait()


def shards(dp_n, tp_n, queries, dkeys, dvals, out_grad, lengths, cartridge, first, second):
    rows, features = queries.shape[1:]
    assert dkeys.shape[2] == WIDTH * tp_n and cartridge.shape[2] == WIDTH
    assert tp_n & (tp_n - 1) == 0
    part = cartridge.shape[0]
    pre = part * dp_n
    dia = rows * tp_n
    total = pre + dia
    halves = dp_n // 2
    scale = WIDTH ** (-0.5)
    sds = jax.ShapeDtypeStruct
    vm = pl.BlockSpec(memory_space=VMEM)
    hbm = pl.BlockSpec(memory_space=pl.ANY)
    dma = lambda n: pltpu.SemaphoreType.DMA((n,))
    block = (2, part, WIDTH)
    tile = (2, rows, WIDTH)
    wide = rows * GROUP

    grad, kvg, qg = pl.pallas_call(
        functools.partial(fused_kernel, dp_n, tp_n, scale),
        out_shape=(
            sds(block, F32), sds((2, rows, dkeys.shape[2]), BF16), sds((rows, features), BF16),
        ),
        in_specs=[pl.BlockSpec(memory_space=pltpu.SMEM)] + [pl.BlockSpec(memory_space=pltpu.HBM)] * 5,
        out_specs=(vm, vm, hbm),
        scratch_shapes=[
            VMEM((part, 2, WIDTH), F32), VMEM(block, BF16),
            VMEM((rows, features), BF16), VMEM((rows, features), BF16), VMEM((rows, features), BF16),
            VMEM((tp_n, dp_n) + block, BF16), VMEM((tp_n, tp_n) + tile, BF16),
            VMEM((WIDTH, total), BF16),
            VMEM((total, WIDTH), F32), VMEM((total, WIDTH), F32),
            *[VMEM((total, wide), F32)] * 6,
            VMEM((tp_n, 2, halves) + block, BF16), VMEM((tp_n, tp_n) + tile, BF16),
            VMEM((tp_n, halves) + block, BF16), VMEM((tp_n, halves) + block, BF16),
            VMEM((tp_n, halves) + block, BF16), VMEM((tp_n,) + block, BF16), VMEM((tp_n,) + block, BF16),
            VMEM((tp_n, tp_n) + tile, BF16), VMEM((tp_n,) + tile, BF16), VMEM((tp_n,) + tile, F32),
            dma(4), dma(2 * tp_n), dma(tp_n), dma(tp_n + tp_n * halves), dma(tp_n * dp_n),
            dma(tp_n * tp_n), dma(tp_n * tp_n), dma(tp_n * tp_n), dma(tp_n * halves),
            dma(tp_n), dma(tp_n), dma(tp_n * halves), dma(tp_n * halves), dma(tp_n), dma(tp_n),
            dma(tp_n * tp_n), dma(tp_n * tp_n), dma(tp_n),
        ],
        compiler_params=pltpu.CompilerParams(
            collective_id=0, has_side_effects=True, vmem_limit_bytes=40 * 2**20,
        ),
        name="fused",
    )(lengths, *[pltpu.with_memory_space_constraint(a, pltpu.HBM) for a in (cartridge, dkeys[0], dvals[0], queries[0], out_grad[0])])

    state = sds((part, 2, WIDTH), F32)
    qg, kg, vg, new_c, new_m, new_v = pl.pallas_call(
        update_kernel,
        out_shape=(
            sds((rows, features), BF16), sds((rows, dkeys.shape[2]), BF16), sds((rows, dkeys.shape[2]), BF16),
            state, state, state,
        ),
        in_specs=[vm] * 6,
        out_specs=(hbm,) * 3 + (vm,) * 3,
        scratch_shapes=[dma(3)],
        compiler_params=pltpu.CompilerParams(vmem_limit_bytes=8 * 2**20),
        name="update",
    )(grad, kvg, qg, cartridge, first, second)
    return (qg[None], kg[None], vg[None], new_c, new_m, new_v)


def solution(mesh):
    tokens = P("dp", "tensor", None)
    prefix = P("dp", None, "tensor")
    return jax.shard_map(
        functools.partial(shards, mesh.shape["dp"], mesh.shape["tensor"]),
        mesh=mesh,
        in_specs=(tokens, tokens, tokens, tokens, P("dp"), prefix, prefix, prefix),
        out_specs=(tokens, tokens, tokens, prefix, prefix, prefix),
        check_vma=False,
    )
```

```python
import functools
import math

import jax
import jax.numpy as jnp
from jax import lax
from jax.experimental import pallas as pl
from jax.experimental.pallas import tpu as pltpu
from jax.sharding import PartitionSpec as P

STEP = 10
BETA_ONE = 0.9
BETA_TWO = 0.999
ADAM_EPS = 1e-08
LEARN_RATE = 0.01
MASKED = -1e30
WIDTH = 128
GROUP = 4
VMEM = pltpu.VMEM
MESH = pl.DeviceIdType.MESH
F32 = jnp.float32
BF16 = jnp.bfloat16


def greet(dp_n, tp_n, me, z):
    barrier = pltpu.get_barrier_semaphore()
    for other in range(1, tp_n):
        pl.semaphore_signal(
            barrier, inc=1, device_id=(me, lax.rem(z + other, tp_n)), device_id_type=MESH
        )
    half, par = me // 2, lax.rem(me, 2)
    pl.semaphore_signal(barrier, inc=1, device_id=(2 * half + 1 - par, z), device_id_type=MESH)
    for other in range(1, dp_n // 2):
        peer = 2 * lax.rem(half + other, dp_n // 2) + par
        pl.semaphore_signal(barrier, inc=1, device_id=(peer, z), device_id_type=MESH)
    return lambda: pl.semaphore_wait(barrier, tp_n - 1 + dp_n // 2)


def fused_kernel(
    dp_n, tp_n, scale, len_ref, cart_hbm, k_hbm, v_hbm, q_hbm, g_hbm, grad_ref, kvg_ref, qg_hbm,
    cart_ref, pre_ref, q_ref, g_ref, qg_ref, gp, gkv, keys_t, dk, dv, sc0, ec0, dc0, sc1, ec1, dc1,
    dpre, ddia, pair_in, pair_sum, plane_in, plane_sum, line_in, dia_in, dia_near, dia_acc,
    local, kv_local, qg_sem, pre_send, pre_recv, kv_send, kv_recv, swap_send, relay,
    pair_send, pair_recv, plane_send, plane_recv, line_send, line_recv, dia_send, dia_recv, near_recv,
):
    sc, ec, dc = (sc0, sc1), (ec0, ec1), (dc0, dc1)
    me, z = lax.axis_index("dp"), lax.axis_index("tensor")
    half, par = me // 2, lax.rem(me, 2)
    halves = dp_n // 2
    partner = 2 * half + 1 - par
    rows = k_hbm.shape[0]
    total = keys_t.shape[1]
    dia = tp_n * rows
    pre = total - dia
    part = pre_ref.shape[1]
    heads = q_ref.shape[1] // WIDTH // tp_n
    assert heads == 2 * GROUP
    wide = rows * GROUP
    chunk = 512
    assert pre % chunk == 0 and chunk % rows == 0 and chunk % pre_ref.shape[1] == 0
    spans = [slice(at, at + chunk) for at in range(0, total, chunk)]

    def remote(src, dst, s, r, to):
        return pltpu.make_async_remote_copy(
            src_ref=src, dst_ref=dst, send_sem=s, recv_sem=r, device_id=to, device_id_type=MESH
        )

    def lanes(k, width):
        return pl.ds(pl.multiple_of(k * width, width), width)

    arrive = greet(dp_n, tp_n, me, z)
    keep = [
        pltpu.make_async_copy(q_hbm, q_ref, local.at[0]),
        pltpu.make_async_copy(g_hbm, g_ref, local.at[1]),
    ] + [
        pltpu.make_async_copy(
            (k_hbm, v_hbm)[w].at[:, k * WIDTH : (k + 1) * WIDTH], gkv.at[k, z, w], kv_local.at[2 * k + w]
        )
        for k in range(tp_n)
        for w in range(2)
    ]
    cart_copy = pltpu.make_async_copy(cart_hbm, cart_ref, local.at[2])
    cart_copy.start()
    for copy in keep[2:] + keep[:2]:
        copy.start()
    cart_copy.wait()
    for w in range(2):
        pre_ref[w] = cart_ref[:, w, :].astype(BF16)
    own_copy = pltpu.make_async_copy(pre_ref, gp.at[z, me], local.at[3])
    own_copy.start()
    for copy in keep[2:]:
        copy.wait()
    keep = keep[:2] + [own_copy]
    arrive()

    bits = tp_n.bit_length() - 1

    def flip(a, b):
        out = 0
        for bit in range(bits):
            u, v = lax.rem(a // 2**bit, 2), lax.rem(b // 2**bit, 2)
            out = out + 2**bit * (u + v - 2 * u * v)
        return out

    def head_at(j):
        at = tp_n - 1 - jnp.int32(j)
        return flip(z, flip(at, at // 2))

    mate = z + 1 - 2 * lax.rem(z, 2)

    def leads(j):
        return (lax.rem(j, 2) == 0) & (j < tp_n - 1)

    def pre_across(j):
        return remote(
            pre_ref, gp.at[z, me], pre_send.at[j], pre_recv.at[z * dp_n + me], (me, head_at(j))
        )

    def pre_forward(t, j):
        return remote(gp.at[t, me], gp.at[t, me], pre_send.at[j + 1], pre_recv.at[t * dp_n + me], (me, mate))

    def pre_spread(t, j, other):
        to = 2 * lax.rem(half + other, halves) + par if other else partner
        return remote(
            gp.at[t, me], gp.at[t, me], pre_send.at[tp_n + j * halves + other], pre_recv.at[t * dp_n + me], (to, z)
        )

    def pre_relay(t, j, other):
        d = 2 * lax.rem(half + halves - other, halves) + par
        return remote(
            gp.at[t, d], gp.at[t, d], relay.at[j * halves + other], pre_recv.at[t * dp_n + d], (partner, z)
        )

    def pre_await(t, d):
        remote(gp.at[t, d], gp.at[t, d], pre_send.at[0], pre_recv.at[t * dp_n + d], (partner, z)).wait_recv()

    def kv_copy(j, other):
        at = tp_n - 1 - jnp.int32(j)
        k = flip(z + other, flip(at, at // 2))
        return remote(
            gkv.at[k, z], gkv.at[k, z], kv_send.at[other * tp_n + j], kv_recv.at[k * tp_n + z], (me, z + other)
        )

    def kv_swap(k, j, b):
        return remote(gkv.at[k, b], gkv.at[k, b], swap_send.at[j * tp_n + b], kv_recv.at[k * tp_n + b], (me, mate))

    def kv_await(k):
        for b in range(tp_n - 1):

            @pl.when(b < z)
            def _():
                at = gkv.at[k, b]
                remote(at, at, kv_send.at[0], kv_recv.at[k * tp_n + b], (partner, z)).wait_recv()

    def kv_send_all(j):
        for other in range(tp_n - 1, 0, -1):

            @pl.when(z + other < tp_n)
            def _():
                kv_copy(j, other).start()

    def swap_all(k, j):
        for b in range(tp_n - 1):

            @pl.when((b < mate) & ((j > 0) | (b != z)))
            def _():
                kv_swap(k, j, b).start()

    for j in range(0, tp_n - 1, 2):
        pre_across(j).start()
        if j == 0:
            pl.when(z > 0)(lambda: kv_send_all(0))
            pl.when((z > 0) & (z < mate))(lambda: kv_swap(head_at(0), 0, z).start())

    for b in range(1, tp_n):

        @pl.when(z < b)
        def _():
            gkv[:, b] = jnp.zeros((tp_n, 2, rows, WIDTH), BF16)

    for copy in keep:
        copy.wait()
    real = z * rows + lax.broadcasted_iota(jnp.int32, (rows, WIDTH), 0) < len_ref[0]
    for at in range(0, g_ref.shape[1], WIDTH):
        at = slice(at, at + WIDTH)
        g_ref[:, at] = jnp.where(real, g_ref[:, at].astype(F32), 0.0).astype(BF16)

    def relay_all(t, j):
        for other in range(1, halves):
            copy = pre_relay(t, j, other)
            copy.wait_recv()
            copy.start()

    def spread_all(j):
        t = head_at(j)
        pl.when(j < tp_n - 1)(lambda: pre_await(t, me))
        pl.when(leads(j) & (j + 1 < tp_n - 1))(lambda: pre_forward(t, j).start())
        for other in list(range(1, halves)) + [0]:
            pre_spread(t, j, other).start()

    spread_all(jnp.int32(0))
    pl.when(z == 0)(lambda: kv_send_all(0))
    pl.when((z == 0) & (z < mate))(lambda: kv_swap(head_at(0), 0, z).start())
    relay_all(head_at(0), 0)
    if tp_n > 1:
        spread_all(jnp.int32(1))

    nt = (((1,), (1,)), ((), ()))
    fold = scale * math.log2(math.e)
    row_pos = z * rows + lax.rem(lax.broadcasted_iota(jnp.int32, (chunk, wide), 1), rows)
    lead = lax.broadcasted_iota(jnp.int32, (chunk, wide), 0) - row_pos

    def take(ref, k, p):
        return jnp.concatenate([ref[:, lanes(k * heads + p * GROUP + i, WIDTH)] for i in range(GROUP)], 0)

    def rows_of(k, w, span):
        if span.start < pre:
            return gp[k, span.start // part : span.stop // part, w].reshape(chunk, WIDTH)
        at = slice((span.start - pre) // rows, (span.stop - pre) // rows)
        return gkv[k, at, w].reshape(chunk, WIDTH)

    def score(k, p, span, q, top):
        s = lax.dot_general(rows_of(k, 0, span), q, nt, preferred_element_type=F32)
        if span.start >= pre:
            s = jnp.where(lead <= pre - span.start, s, MASKED)
        sc[p][span] = s
        return jnp.maximum(top, jnp.max(s, axis=0, keepdims=True))

    def weigh(k, p, span, g, top, norm, mix):
        e = jnp.exp2((sc[p][span] - top) * fold)
        d = lax.dot_general(rows_of(k, 1, span), g, nt, preferred_element_type=F32)
        ec[p][span] = e
        dc[p][span] = d
        return norm + jnp.sum(e, axis=0, keepdims=True), mix + jnp.sum(e * d, axis=0, keepdims=True)

    def grads(p, span, q, g, inv, row_dot, qt):
        w = ec[p][span] * inv
        ds = (w * (dc[p][span] - row_dot)).astype(BF16)
        more_v = jnp.dot(w.astype(BF16), g, preferred_element_type=F32)
        more_k = jnp.dot(ds, q, preferred_element_type=F32)
        if p == 0:
            dv[span] = more_v
            dk[span] = more_k
        else:
            dv[span] += more_v
            dk[span] += more_k
        return qt + jnp.dot(keys_t[:, span], ds, preferred_element_type=F32)

    def put(k, p, qt):
        qt = qt * scale
        for i in range(GROUP):
            qg_ref[:, lanes(k * heads + p * GROUP + i, WIDTH)] = (
                qt[:, i * rows : (i + 1) * rows].T.astype(BF16)
            )

    def attend(j, k):
        none = jnp.zeros((1, wide), F32)
        low = jnp.full((1, wide), MASKED, F32)
        q, g = [take(q_ref, k, p) for p in range(2)], [take(g_ref, k, p) for p in range(2)]
        top = [low, low]
        norm, mix = [none, none], [none, none]
        qt = [jnp.zeros((WIDTH, wide), F32)] * 2
        for span in spans:
            top[0] = score(k, 0, span, q[0], top[0])
        for span in spans:
            norm[0], mix[0] = weigh(k, 0, span, g[0], top[0], norm[0], mix[0])
            top[1] = score(k, 1, span, q[1], top[1])
        inv = 1.0 / norm[0]
        row_dot = mix[0] * inv
        def kv_ahead():
            kv_await(head_at(j + 1))
            swap_all(head_at(j + 1), j + 1)

        pl.when(leads(j + 1) & (j > 0))(kv_ahead)
        pl.when(j > 1)(lambda: to_line(j - 2))
        pl.when(j > 0)(lambda: to_plane(j - 1))
        pl.when(j + 2 < tp_n)(lambda: spread_all(j + 2))
        q, g = [take(q_ref, k, p) for p in range(2)], [take(g_ref, k, p) for p in range(2)]
        for span in spans[::-1]:
            norm[1], mix[1] = weigh(k, 1, span, g[1], top[1], norm[1], mix[1])
            qt[0] = grads(0, span, q[0], g[0], inv, row_dot, qt[0])
        put(k, 0, qt[0])
        inv = 1.0 / norm[1]
        row_dot = mix[1] * inv
        late = [span for span in spans if span.start >= pre]
        early = [span for span in spans if span.start < pre]
        for span in late:
            qt[1] = grads(1, span, q[1], g[1], inv, row_dot, qt[1])
        pl.when(j + 1 < tp_n)(lambda: relay_all(head_at(j + 1), j + 1))
        leave_dia(j)
        if tp_n > 1:
            pl.when((j == tp_n - 1) & (z > mate))(lambda: dia_join(tp_n - 1))
        for span in early:
            qt[1] = grads(1, span, q[1], g[1], inv, row_dot, qt[1])
        put(k, 1, qt[1])
        leave_pre(j)

    def qg_copy(j):
        at = lanes(head_at(j), heads * WIDTH)
        return pltpu.make_async_copy(qg_ref.at[:, at], qg_hbm.at[:, at], qg_sem.at[j])

    def pair_copy(j):
        return remote(dpre.at[j, 1 - par], pair_in.at[j], pair_send.at[j], pair_recv.at[j], (partner, z))

    def plane_copy(j, other):
        to = lax.rem(half + other, halves)
        at = j * halves + other
        return remote(
            pair_sum.at[j, to], plane_in.at[j, other], plane_send.at[at], plane_recv.at[at],
            (2 * to + par, z),
        )

    def line_copy(j):
        return remote(
            plane_sum.at[j], line_in.at[j], line_send.at[j], line_recv.at[j],
            (me, jnp.where(leads(j), mate, head_at(j))),
        )

    def led_by(j):
        return j - 1

    def line_take(j):
        remote(line_in.at[j], line_in.at[j], line_send.at[j], line_recv.at[j], (partner, z)).wait_recv()
        return line_in[j].astype(F32)

    def dia_trade(j, b):
        return remote(
            ddia.at[j, b], dia_near.at[b], dia_send.at[j * tp_n + b], near_recv.at[b], (me, mate)
        )

    def dia_copy(j, b):
        k = head_at(j)
        return remote(
            ddia.at[j, b], dia_in.at[z, k], dia_send.at[j * tp_n + b], dia_recv.at[z * tp_n + k], (me, b)
        )

    def leave_dia(j):
        for b in range(tp_n):
            at = slice(pre + b * rows, pre + (b + 1) * rows)
            ddia[j, b, 0] = (dk[at] * scale).astype(BF16)
            ddia[j, b, 1] = dv[at].astype(BF16)
        for b in range(tp_n - 1):
            pl.when((b < z) & (j == tp_n - 2))(lambda: dia_trade(j, b).start())
            pl.when((b < z) & (j < tp_n - 2))(lambda: dia_copy(j, b).start())

    def leave_pre(j):
        for d in range(dp_n):
            at = slice(d * part, (d + 1) * part)
            dpre[j, d % 2, d // 2, 0] = (dk[at] * scale).astype(BF16)
            dpre[j, d % 2, d // 2, 1] = dv[at].astype(BF16)
        pair_copy(j).start()
        qg_copy(j).start()

    def dia_join(j):
        for b in range(tp_n - 1):

            @pl.when(b < mate)
            def _():
                dia_trade(j - 1, b).wait_recv()
                ddia[j, b] = (ddia[j, b].astype(F32) + dia_near[b].astype(F32)).astype(BF16)

            pl.when(b < z)(lambda: dia_copy(j, b).start())

    def to_plane(j):
        pair_copy(j).wait_recv()
        for other in list(range(1, halves)) + [0]:
            to = lax.rem(half + other, halves)
            pair_sum[j, to] = (dpre[j, par, to].astype(F32) + pair_in[j, to].astype(F32)).astype(BF16)
            if other:
                plane_copy(j, other).start()

    def plane_total(j):
        acc = pair_sum[j, half].astype(F32)
        for other in range(1, halves):
            plane_copy(j, other).wait_recv()
            acc += plane_in[j, other].astype(F32)
        return acc

    def to_line(j):
        acc = plane_total(j)

        @pl.when(leads(j))
        def _():
            plane_sum[j] = acc.astype(BF16)
            line_copy(j).start()

        @pl.when(jnp.logical_not(leads(j)) & (j < tp_n - 1))
        def _():
            plane_sum[j] = (acc + line_take(led_by(j))).astype(BF16)
            line_copy(j).start()

        @pl.when(j == tp_n - 1)
        def _():
            grad_ref[...] = acc + line_take(led_by(j)) if tp_n > 1 else acc

    @pl.loop(0, tp_n)
    def _(j):
        k = head_at(j)
        for other in range(halves):
            pre_await(k, 2 * lax.rem(half + other, halves) + 1 - par)
        pl.when((j == 0) | (lax.rem(j, 2) == 1))(lambda: kv_await(k))
        pl.when(j == 0)(lambda: swap_all(k, j))
        pl.when(leads(j) & (j + 2 < tp_n - 1))(lambda: kv_send_all(j + 2))
        for span in spans:
            keys_t[:, span] = rows_of(k, 0, span).T

        attend(j, k)

    to_plane(tp_n - 1)
    if tp_n > 1:
        to_line(jnp.int32(tp_n - 2))
    if tp_n > 1:
        pl.when(z < mate)(lambda: dia_join(tp_n - 1))
    to_line(jnp.int32(tp_n - 1))

    def own_dia(k):
        gray = flip(jnp.int32(k), z)
        j = gray
        for bit in range(1, bits):
            j = flip(j, gray // 2**bit)
        return ddia[tp_n - 1 - j, z].astype(F32)

    for k in range(tp_n):
        dia_acc[k] = own_dia(k)
    for b in range(1, tp_n):

        @pl.when(z < b)
        def _():
            for j in range(tp_n):
                if j != tp_n - 2:
                    k = flip(jnp.int32(b), flip(z, head_at(j)))
                    at = dia_in.at[b, k]
                    remote(at, at, dia_send.at[0], dia_recv.at[b * tp_n + k], (partner, z)).wait_recv()
                    dia_acc[k] += dia_in[b, k].astype(F32)

    for k in range(tp_n):
        at = slice(k * WIDTH, (k + 1) * WIDTH)
        kvg_ref[0, :, at] = dia_acc[k, 0].astype(BF16)
        kvg_ref[1, :, at] = dia_acc[k, 1].astype(BF16)

    for j in range(1, tp_n - 1, 2):
        grad_ref[...] += line_take(j)

    @pl.loop(0, tp_n)
    def _(j):
        qg_copy(j).wait()
        pair_copy(j).wait_send()
        for other in range(halves):
            pre_spread(z, j, other).wait_send()
        for other in range(1, halves):
            plane_copy(j, other).wait_send()
            pre_relay(z, j, other).wait_send()
        for b in range(tp_n - 1):

            @pl.when(b < z)
            def _():
                dia_copy(j, b).wait_send()

        for other in range(1, tp_n):

            @pl.when((z + other < tp_n) & leads(j))
            def _():
                kv_copy(j, other).wait_send()

        for b in range(tp_n - 1):

            @pl.when((b < mate) & leads(j))
            def _():
                kv_swap(head_at(j), j, b).wait_send()

        @pl.when(leads(j))
        def _():
            pre_across(j).wait_send()

        @pl.when(leads(j) & (j + 1 < tp_n - 1))
        def _():
            pre_forward(z, j).wait_send()

        @pl.when(j < tp_n - 1)
        def _():
            line_copy(j).wait_send()


def update_kernel(
    grad_ref, kvg_ref, qg_in, c_ref, m_ref, v_ref, qg_out, kg_ref, vg_ref, nc_ref, nm_ref, nv_ref, sem
):
    out = pltpu.make_async_copy(qg_in, qg_out, sem.at[0])
    out.start()
    halves = [pltpu.make_async_copy(kvg_ref.at[w], (kg_ref, vg_ref)[w], sem.at[1 + w]) for w in range(2)]
    for copy in halves:
        copy.start()
    for w in range(2):
        grad = grad_ref[w]
        new_m = BETA_ONE * m_ref[:, w, :] + (1.0 - BETA_ONE) * grad
        new_v = BETA_TWO * v_ref[:, w, :] + (1.0 - BETA_TWO) * grad * grad
        update = new_m / (1.0 - BETA_ONE**STEP) / (jnp.sqrt(new_v / (1.0 - BETA_TWO**STEP)) + ADAM_EPS)
        nc_ref[:, w, :] = c_ref[:, w, :] - LEARN_RATE * update
        nm_ref[:, w, :] = new_m
        nv_ref[:, w, :] = new_v
    for copy in halves + [out]:
        copy.wait()


def shards(dp_n, tp_n, queries, dkeys, dvals, out_grad, lengths, cartridge, first, second):
    rows, features = queries.shape[1:]
    assert dkeys.shape[2] == WIDTH * tp_n and cartridge.shape[2] == WIDTH
    assert tp_n & (tp_n - 1) == 0
    part = cartridge.shape[0]
    pre = part * dp_n
    dia = rows * tp_n
    total = pre + dia
    halves = dp_n // 2
    scale = WIDTH ** (-0.5)
    sds = jax.ShapeDtypeStruct
    vm = pl.BlockSpec(memory_space=VMEM)
    hbm = pl.BlockSpec(memory_space=pl.ANY)
    dma = lambda n: pltpu.SemaphoreType.DMA((n,))
    block = (2, part, WIDTH)
    tile = (2, rows, WIDTH)
    wide = rows * GROUP

    grad, kvg, qg = pl.pallas_call(
        functools.partial(fused_kernel, dp_n, tp_n, scale),
        out_shape=(
            sds(block, F32), sds((2, rows, dkeys.shape[2]), BF16), sds((rows, features), BF16),
        ),
        in_specs=[pl.BlockSpec(memory_space=pltpu.SMEM)] + [pl.BlockSpec(memory_space=pltpu.HBM)] * 5,
        out_specs=(vm, vm, hbm),
        scratch_shapes=[
            VMEM((part, 2, WIDTH), F32), VMEM(block, BF16),
            VMEM((rows, features), BF16), VMEM((rows, features), BF16), VMEM((rows, features), BF16),
            VMEM((tp_n, dp_n) + block, BF16), VMEM((tp_n, tp_n) + tile, BF16),
            VMEM((WIDTH, total), BF16),
            VMEM((total, WIDTH), F32), VMEM((total, WIDTH), F32),
            *[VMEM((total, wide), F32)] * 6,
            VMEM((tp_n, 2, halves) + block, BF16), VMEM((tp_n, tp_n) + tile, BF16),
            VMEM((tp_n, halves) + block, BF16), VMEM((tp_n, halves) + block, BF16),
            VMEM((tp_n, halves) + block, BF16), VMEM((tp_n,) + block, BF16), VMEM((tp_n,) + block, BF16),
            VMEM((tp_n, tp_n) + tile, BF16), VMEM((tp_n,) + tile, BF16), VMEM((tp_n,) + tile, F32),
            dma(4), dma(2 * tp_n), dma(tp_n), dma(tp_n + tp_n * halves), dma(tp_n * dp_n),
            dma(tp_n * tp_n), dma(tp_n * tp_n), dma(tp_n * tp_n), dma(tp_n * halves),
            dma(tp_n), dma(tp_n), dma(tp_n * halves), dma(tp_n * halves), dma(tp_n), dma(tp_n),
            dma(tp_n * tp_n), dma(tp_n * tp_n), dma(tp_n),
        ],
        compiler_params=pltpu.CompilerParams(
            collective_id=0, has_side_effects=True, vmem_limit_bytes=40 * 2**20,
        ),
        name="fused",
    )(lengths, *[pltpu.with_memory_space_constraint(a, pltpu.HBM) for a in (cartridge, dkeys[0], dvals[0], queries[0], out_grad[0])])

    state = sds((part, 2, WIDTH), F32)
    qg, kg, vg, new_c, new_m, new_v = pl.pallas_call(
        update_kernel,
        out_shape=(
            sds((rows, features), BF16), sds((rows, dkeys.shape[2]), BF16), sds((rows, dkeys.shape[2]), BF16),
            state, state, state,
        ),
        in_specs=[vm] * 6,
        out_specs=(hbm,) * 3 + (vm,) * 3,
        scratch_shapes=[dma(3)],
        compiler_params=pltpu.CompilerParams(vmem_limit_bytes=8 * 2**20),
        name="update",
    )(grad, kvg, qg, cartridge, first, second)
    return (qg[None], kg[None], vg[None], new_c, new_m, new_v)


def solution(mesh):
    tokens = P("dp", "tensor", None)
    prefix = P("dp", None, "tensor")
    return jax.shard_map(
        functools.partial(shards, mesh.shape["dp"], mesh.shape["tensor"]),
        mesh=mesh,
        in_specs=(tokens, tokens, tokens, tokens, P("dp"), prefix, prefix, prefix),
        out_specs=(tokens, tokens, tokens, prefix, prefix, prefix),
        check_vma=False,
    )
```
